256 devices in a mesh: dp: 64 (over y, z_hi, x), mp: 4 (over z_lo, core).
Axes of the slice: x: 4, y: 4, z: 8 (z_hi: 4, z_lo: 2; z = z_hi * 2 + z_lo), core: 2. Of those that a mesh axis runs over, the one named last changes fastest.
Arguments:
- tokens: bfloat16 [4096, 2, 3072], P('dp'), may hold values from -6 to 6
- norm_gain_vector: float32 [3072], replicated, may hold values from 0.5 to 1.5
- query_weight: bfloat16 [3072, 1536], P('dp', 'mp'), may hold values from -0.109375 to 0.109375
- key_weight: bfloat16 [3072, 1536], P('dp', 'mp'), may hold values from -0.4375 to 0.4375
- value_weight: bfloat16 [3072, 1536], P('dp', 'mp'), may hold values from -0.109375 to 0.109375
- output_weight: bfloat16 [3072, 1536], P('dp', 'mp'), may hold values from -0.15625 to 0.15625
- prefix_cache: bfloat16 [64, 64, 2, 1536], P('dp', None, None, 'mp'), may hold values from -64 to 64
- lengths: int32 [4096], P('dp'), may hold values from 1 to 2, 5120 in all
- groups: int32 [4096], P('dp'), may hold values from 0 to 3
- deal_slot: int32 [4096], P('dp'), may hold values from 0 to 4095, as said below
- owners: int32 [64], replicated, may hold values from 0 to 63, each once
Outputs:
- hidden: bfloat16 [4096, 2, 3072], P('dp', None, 'mp')
- suffix_cache: bfloat16 [4096, 2, 2, 1536], P('dp', None, None, 'mp')
The draws below stay inside these ranges and needn't reach their ends.
Inputs may be any that keep to these rules, and one draw needn't show every extreme that they name: Every value once; the 64 requests that start on one index of dp go to 64 different devices deal_slot // 64, one to each.
All inputs are finite; a program needn't handle non-finite values. No bound on the sum of `lengths` on one device may be relied on, other than what follows from the above.
Results may differ from the reference program's by a relative error of at most 0.013.
The reference program's roundings to bfloat16 on the way count: a program that leaves them out, or rounds other values in their place, can miss the bound.
Values may be sent and summed in bfloat16 or wider, within the bound.
No kernel may reach another device: no remote copies, remote signals or barrier semaphores. Data moves between devices by JAX's collectives and lax.ppermute only.
A program may use at most 128 MiB of HBM per device.

```python
import math
import jax
import jax.numpy as jnp
import numpy as np
from jax import lax

D = 3072
HEADS = 16
HD = 96
GROUPS = 4
SLOT = 2
PBLK = 64
HQ = 1536
REQ_DEV = 64
REQUESTS = 4096
BLOCKS = 16
PREFIX = 1024
LIVE = 5120


def draw_deal_slot(key, part):
    key_first, key_second = jax.random.split(key)
    send_dest = jax.vmap(lambda key_item: jax.random.permutation(key_item, REQ_DEV))(jax.random.split(key_first, REQ_DEV)).astype(jnp.int32)
    land_slot = jax.vmap(lambda key_item: jax.random.permutation(key_item, REQ_DEV))(jax.random.split(key_second, REQ_DEV)).astype(jnp.int32)
    source_ids = jnp.broadcast_to(jnp.arange(REQ_DEV, dtype=jnp.int32)[:, None], (REQ_DEV, REQ_DEV))
    slot_index = land_slot[send_dest, source_ids]
    return (send_dest * REQ_DEV + slot_index).reshape(REQUESTS).astype(jnp.int32)


def draw_prefix_cache(key, part):
    key_first = jax.random.fold_in(key, 0)
    draw_shape = (GROUPS * BLOCKS, PBLK, 2, HQ)
    kind_scale = jnp.array([1.5, 1.0], jnp.float32)[None, None, :, None]
    result_rows = jax.random.normal(key_first, draw_shape, jnp.float32) * kind_scale
    return jnp.clip(result_rows, -64.0, 64.0).astype(jnp.bfloat16)


def place_ends(entries, own_key, low, top_value):
    place = [jax.random.randint(jax.random.fold_in(own_key, axis), (), 0, length) for axis, length in enumerate(entries.shape)]
    widest = entries.shape.index(max(entries.shape))
    beside = place[:widest] + [(place[widest] + 1) % entries.shape[widest]] + place[widest + 1:]
    return entries.at[tuple(place)].set(low).at[tuple(beside)].set(top_value)


def shard_levels(key, shape, cuts, low, largest):
    def one(dim, shards_of):
        steps = jax.random.uniform(jax.random.fold_in(jax.random.fold_in(key, 6), dim), (shards_of,), jnp.float32, low / len(cuts), largest / len(cuts))
        return jnp.repeat(jnp.exp(steps), shape[dim] // shards_of).reshape((-1,) + (1,) * (len(shape) - dim - 1))

    gain = one(*cuts[0])
    for cut in cuts[1:]:
        gain = gain * one(*cut)
    return gain


def length_profile(amount, total, reach, slope):
    loads = [(1 << 20) // math.isqrt(rank ** slope) + 1 for rank in range(2, amount + 1)]
    rest, counts = total - reach - (amount - 1), [1] * (amount - 1)
    while rest > 0:
        movable = [i for i in range(amount - 1) if counts[i] < reach]
        mass, left = sum([loads[i] for i in movable]), rest
        for i in movable:
            extra = min(reach - counts[i], max(1, left * loads[i] // mass), rest)
            counts[i] = counts[i] + extra
            rest = rest - extra
    return np.array([reach] + counts)


def uneven(stream_key, amount, total, bound, slope):
    if amount == 2:
        one = jax.random.randint(stream_key, (), max(1, total - bound), min(bound, total - 1) + 1)
        return jnp.stack([one, total - one])
    sizes = jnp.asarray(length_profile(amount, total, bound, slope), jnp.int32)
    couples = (amount - 1) // 2
    source_of, sink = sizes[1:1 + 2 * couples:2], sizes[2:2 + 2 * couples:2]
    room = jnp.minimum(source_of - 1, bound - sink)
    shifted = jax.random.randint(jax.random.fold_in(stream_key, 1), (couples,), 0, 1 << 20) % (room + 1)
    sizes = sizes.at[1:1 + 2 * couples:2].set(source_of - shifted).at[2:2 + 2 * couples:2].set(sink + shifted)
    return sizes[jax.random.permutation(jax.random.fold_in(stream_key, 2), amount)]


def noise(stream_key, dims, deviation, bound, cuts=(), held_as=jnp.bfloat16):
    drawn = deviation * jax.random.normal(stream_key, dims, jnp.float32)
    if cuts:
        drawn = drawn * shard_levels(stream_key, dims, cuts, -0.22, 0.18)
    return jnp.clip(drawn, -bound, bound).astype(held_as)


def setup_inputs(seed: int = 0) -> dict:
    splits = jax.random.split(jax.random.key(seed), 12)
    return {
        "tokens": noise(splits[0], (REQUESTS, SLOT, D), 1.0, 6.0, ((0, 64),)),
        "norm_gain_vector": jnp.clip(1.0 + 0.1 * jax.random.normal(splits[1], (D,), jnp.float32), 0.5, 1.5),
        "query_weight": noise(splits[2], (D, HQ), D ** -0.5, 0.109375, ((0, 64), (1, 4))),
        "key_weight": noise(splits[3], (D, HQ), (D // 16) ** -0.5, 0.4375, ((0, 64), (1, 4))),
        "value_weight": noise(splits[4], (D, HQ), D ** -0.5, 0.109375, ((0, 64), (1, 4))),
        "output_weight": noise(splits[5], (D, HQ), HQ ** -0.5, 0.15625, ((0, 64), (1, 4))),
        "prefix_cache": draw_prefix_cache(jax.random.fold_in(splits[11], 71), 0),
        "lengths": uneven(splits[7], REQUESTS, LIVE, SLOT, 1).astype(jnp.int32),
        "groups": place_ends(jax.random.randint(splits[8], (REQUESTS,), 0, GROUPS), jax.random.fold_in(splits[8], 1), 0, GROUPS - 1).astype(jnp.int32),
        "deal_slot": draw_deal_slot(jax.random.fold_in(splits[11], 71), 0),
        "owners": jax.random.permutation(splits[10], GROUPS * BLOCKS).astype(jnp.int32),
    }


def rope_tables(slot_len, head_dim, first_pos):
    position = (first_pos + jnp.arange(slot_len)).astype(jnp.float32)
    frequency = 10000.0 ** (-jnp.arange(head_dim // 2).astype(jnp.float32) * 2.0 / head_dim)
    angles = position[:, None] * frequency[None, :]
    angles = jnp.concatenate([angles, angles], axis=-1)
    return (jnp.cos(angles)[:, None, :], jnp.sin(angles)[:, None, :])

def rope_rotate(values, cosine, sine_table):
    half_dim = values.shape[-1] // 2
    turned = jnp.concatenate([-values[..., half_dim:], values[..., :half_dim]], axis=-1)
    return values * cosine + turned * sine_table

def finalize_output(values):
    return lax.optimization_barrier(values.astype(jnp.bfloat16))

def reference(tokens, norm_gain_vector, query_weight, key_weight, value_weight, output_weight, prefix_cache, lengths, groups, deal_slot, owners):
    widened_rows = tokens.astype(jnp.float32)
    reciprocal_root_scale = lax.rsqrt(lax.optimization_barrier(jnp.mean(widened_rows * widened_rows, axis=-1, keepdims=True)) + 1e-05)
    normalized_rows = finalize_output(widened_rows * reciprocal_root_scale * norm_gain_vector)
    flat_rows = normalized_rows.reshape(REQUESTS * SLOT, D)
    cosine, sine_table = rope_tables(SLOT, HD, PREFIX)

    def head_split(matrix, rotate_it):
        result_rows = jnp.dot(flat_rows, matrix, preferred_element_type=jnp.float32).reshape(REQUESTS, SLOT, HEADS, HD)
        if rotate_it:
            result_rows = rope_rotate(result_rows, cosine, sine_table)
        return finalize_output(result_rows)
    queries = head_split(query_weight, True)
    keyed = head_split(key_weight, True)
    valued = head_split(value_weight, False)
    by_group = prefix_cache[owners].reshape(GROUPS, PREFIX, 2, HEADS, HD)
    inv_scale = 1.0 / math.sqrt(HD)
    position = jnp.arange(SLOT)

    def attend_one(request_item):
        query_rows, key_rows, value_rows, length_one, group_one = request_item
        group_cache = lax.dynamic_index_in_dim(by_group, group_one, 0, keepdims=False)
        all_keys = jnp.concatenate([group_cache[:, 0], key_rows], axis=0).astype(jnp.float32)
        all_values = jnp.concatenate([group_cache[:, 1], value_rows], axis=0).astype(jnp.float32)
        scores = jnp.einsum('thd,khd->htk', query_rows.astype(jnp.float32), all_keys) * inv_scale
        suffix_ok = (position[:, None] >= position[None, :]) & (position[None, :] < length_one)
        allowed = jnp.concatenate([jnp.ones((SLOT, PREFIX), bool), suffix_ok], axis=1)[None]
        scores = jnp.where(allowed, scores, -jnp.inf)
        peak = lax.optimization_barrier(jnp.max(scores, axis=-1, keepdims=True))
        weights = jnp.exp(scores - peak)
        run_sum = lax.optimization_barrier(jnp.sum(weights, axis=-1, keepdims=True))
        probs = finalize_output(weights).astype(jnp.float32)
        mixed = jnp.einsum('htk,khd->thd', probs, all_values) / jnp.transpose(run_sum, (1, 0, 2))
        return mixed.astype(jnp.bfloat16).reshape(SLOT, HQ)
    attended = lax.map(attend_one, (queries, keyed, valued, lengths, groups))
    projected = jnp.dot(attended.reshape(REQUESTS * SLOT, HQ), output_weight.T, preferred_element_type=jnp.float32)
    live_mask = (position[None, :] < lengths[:, None]).reshape(REQUESTS * SLOT, 1)
    hidden = jnp.where(live_mask, projected, 0.0).astype(jnp.bfloat16).reshape(REQUESTS, SLOT, D)
    stacked_parts = jnp.stack([keyed.reshape(REQUESTS, SLOT, HQ), valued.reshape(REQUESTS, SLOT, HQ)], axis=2)
    stacked_parts = jnp.where(live_mask.reshape(REQUESTS, SLOT, 1, 1), stacked_parts, jnp.zeros_like(stacked_parts))
    suffix_cache = jnp.zeros_like(stacked_parts).at[deal_slot].set(stacked_parts)
    return (hidden, suffix_cache)
```

```python
import functools
import math

import jax
import jax.numpy as jnp
import numpy as np
from jax import lax
from jax.experimental import pallas as pl
from jax.experimental.pallas import tpu as pltpu
from jax.sharding import PartitionSpec as P

HD = 96
GROUPS = 4
PBLK = 64
PREFIX = 1024
NEG = -1e30


def dp_shift(axis, amount):
    stride = {"y": 16, "zh": 4, "x": 1}[axis]
    perm = []
    for i in range(64):
        at = (i // stride) % 4
        perm.append((i, i + (((at + amount) % 4) - at) * stride))
    return perm


def shift(value, axis, amount):
    return lax.ppermute(value, "dp", dp_shift(axis, amount))


def mp_xor(value, mask):
    return lax.ppermute(value, "mp", [(i, i ^ mask) for i in range(4)])


def swap_y_mp(value):
    perm = []
    for i in range(64):
        y, rest = divmod(i, 16)
        for m in range(4):
            perm.append((i * 4 + m, (m * 16 + rest) * 4 + y))
    return lax.ppermute(value, ("dp", "mp"), perm)


def dot_nt(a, b):
    return lax.dot_general(a, b, (((1,), (1,)), ((), ())), preferred_element_type=jnp.float32)


def dot_tn(a, b):
    return lax.dot_general(a, b, (((0,), (0,)), ((), ())), preferred_element_type=jnp.float32)


def rope_tables():
    position = (PREFIX + np.arange(2)).astype(np.float32)
    frequency = np.float32(10000.0) ** (-np.arange(HD // 2).astype(np.float32) * np.float32(2.0) / np.float32(HD))
    angles = position[:, None] * frequency.astype(np.float32)[None, :]
    angles = np.concatenate([angles, angles], axis=-1).astype(np.float32)
    return np.cos(angles).astype(np.float32), np.sin(angles).astype(np.float32)


def qkv_kernel(
    pos_ref, own_ref, oth_ref, w0, w1, w2, w3, cos_ref, sin_ref,
    q_out, k_out, v_out, info_out, send_out, wsc,
):
    y, zh, x, c = pos_ref[0], pos_ref[1], pos_ref[2], pos_ref[3]
    for kx, piece in enumerate((w0, w1, w2, w3)):
        xa = (x - kx) & 3
        for kz in range(4):
            wsc[(zh - kz) & 3, xa] = piece[kz]
    accs = [None, None]
    for ky in range(4):
        ya = (y - ky) & 3
        lanes = pl.ds(pl.multiple_of(ya * 768, 128), 768)
        rhs = wsc[:, :, :, 288 * ky : 288 * ky + 288].reshape(768, 288)
        for i, ref in enumerate((own_ref, oth_ref)):
            part = jnp.dot(
                ref[:, :, lanes].reshape(256, 768), rhs, preferred_element_type=jnp.float32
            )
            accs[i] = part if accs[i] is None else accs[i] + part
    first = c == 0
    slots = (jnp.where(first, accs[0], accs[1]), jnp.where(first, accs[1], accs[0]))

    def rotate(values, t):
        turned = jnp.concatenate([-values[:, 48:], values[:, :48]], axis=1)
        return (values * cos_ref[t : t + 1, :] + turned * sin_ref[t : t + 1, :]).astype(jnp.bfloat16)

    info = own_ref[:, :, 3072:3200].reshape(256, 128).astype(jnp.float32)
    info_out[...] = info
    live = info[:, 2:3] > 1.5
    parts = []
    for t in range(2):
        rows = pl.ds(256 * t, 256)
        q_out[rows, :] = rotate(slots[t][:, :96], t)
        keyed = rotate(slots[t][:, 96:192], t)
        valued = slots[t][:, 192:288].astype(jnp.bfloat16)
        k_out[rows, :] = keyed
        v_out[rows, :] = valued
        if t == 1:
            keyed = jnp.where(live, keyed.astype(jnp.float32), 0.0).astype(jnp.bfloat16)
            valued = jnp.where(live, valued.astype(jnp.float32), 0.0).astype(jnp.bfloat16)
        parts += [keyed, valued]
    packed = jnp.concatenate(parts, axis=1)
    dest_iota = lax.broadcasted_iota(jnp.int32, (64, 64), 1).astype(jnp.float32)
    lane_iota = lax.broadcasted_iota(jnp.int32, (64, 128), 1)
    extras = jnp.zeros((64, 128), jnp.float32)
    for ky in range(4):
        block = info[64 * ky : 64 * ky + 64]
        pick = jnp.where(block[:, 0:1] == dest_iota, 1.0, 0.0).astype(jnp.bfloat16)
        moved = dot_tn(pick, packed[64 * ky : 64 * ky + 64])
        send_out[:, 384 * ky : 384 * ky + 384] = moved.astype(jnp.bfloat16)
        slot = jnp.where(lane_iota == ky, block[:, 1:2], 0.0).astype(jnp.bfloat16)
        extras = extras + dot_tn(pick, slot)
    send_out[:, 1536:1664] = extras.astype(jnp.bfloat16)


def attend_kernel(q_ref, k_ref, v_ref, info_ref, kg_ref, p0, p1, p2, p3, out_ref, s_ref):
    factor = math.log2(math.e) / math.sqrt(HD)
    pieces = (p0, p1, p2, p3)
    group = info_ref[:, 3:4]
    live = info_ref[:, 2:3] > 1.5
    for t in range(2):
        rows = pl.ds(256 * t, 256)
        queries = q_ref[rows, :]
        wide = queries.astype(jnp.float32)
        top = jnp.sum(wide * k_ref[0:256, :].astype(jnp.float32), axis=1, keepdims=True)
        selfs = [top]
        if t == 1:
            other = jnp.sum(wide * k_ref[256:512, :].astype(jnp.float32), axis=1, keepdims=True)
            other = jnp.where(live, other, NEG)
            selfs.append(other)
            top = jnp.maximum(top, other)
        for ky in range(4):
            keys = jnp.concatenate(
                [p[:, :, 192 * ky : 192 * ky + 96].reshape(256, 96) for p in pieces], axis=0
            )
            scores = dot_nt(queries, keys)
            scores = jnp.where(group == kg_ref[ky : ky + 1, :], scores, NEG)
            s_ref[ky] = scores
            top = jnp.maximum(top, jnp.max(scores, axis=1, keepdims=True))
        total = jnp.zeros((256, 1), jnp.float32)
        acc = jnp.zeros((256, 96), jnp.float32)
        for i, score in enumerate(selfs):
            weight = jnp.exp2((score - top) * factor)
            total = total + weight
            values = v_ref[256 * i : 256 * i + 256, :].astype(jnp.float32)
            acc = acc + weight.astype(jnp.bfloat16).astype(jnp.float32) * values
        for ky in range(4):
            weights = jnp.exp2((s_ref[ky] - top) * factor)
            total = total + jnp.sum(weights, axis=1, keepdims=True)
            values = jnp.concatenate(
                [p[:, :, 192 * ky + 96 : 192 * ky + 192].reshape(256, 96) for p in pieces], axis=0
            )
            acc = acc + jnp.dot(
                weights.astype(jnp.bfloat16), values, preferred_element_type=jnp.float32
            )
        out_ref[rows, :] = (acc / total).astype(jnp.bfloat16)


def order_kernel(pos_ref, w0, w1, w2, w3, out_ref):
    y, zh, x = pos_ref[0], pos_ref[1], pos_ref[2]
    for ky, piece in enumerate((w0, w1, w2, w3)):
        for kx in range(4):
            for kz in range(4):
                out_ref[(y - ky) & 3, (zh - kz) & 3, (x - kx) & 3] = piece[kx, kz]


def out_kernel(pos_ref, a0, a1, a2, a3, w_ref, len_ref, out_ref):
    m = pos_ref[4]
    acc = None
    for k, block in enumerate((a0, a1, a2, a3)):
        weight = w_ref[m ^ k].reshape(768, 384)
        part = dot_nt(block[...].reshape(128, 384), weight)
        acc = part if acc is None else acc + part
    out_ref[:, 0:768] = acc[0:64].astype(jnp.bfloat16)
    out_ref[:, 768:1536] = jnp.where(len_ref[...] > 1, acc[64:128], 0.0).astype(jnp.bfloat16)


def unpack_kernel(recv_ref, out_ref):
    slot_iota = lax.broadcasted_iota(jnp.int32, (64, 64), 1).astype(jnp.float32)
    for head in range(4):
        rows = pl.ds(16 * head, 16)
        data = jnp.concatenate(
            [recv_ref[rows, 384 * ky : 384 * ky + 384] for ky in range(4)], axis=0
        )
        tail = recv_ref[rows, 1536:1664].astype(jnp.float32)
        slots = jnp.concatenate([tail[:, ky : ky + 1] for ky in range(4)], axis=0)
        pick = jnp.where(slots == slot_iota, 1.0, 0.0).astype(jnp.bfloat16)
        moved = dot_tn(pick, data).astype(jnp.bfloat16)
        for part in range(4):
            out_ref[:, 384 * part + 96 * head : 384 * part + 96 * head + 96] = moved[
                :, 96 * part : 96 * part + 96
            ]


def call(kernel, outs, inputs, scratch=(), scalars=0):
    vmem = pl.BlockSpec(memory_space=pltpu.VMEM)
    smem = pl.BlockSpec(memory_space=pltpu.SMEM)
    single = not isinstance(outs, (list, tuple))
    return pl.pallas_call(
        kernel,
        out_shape=outs,
        in_specs=[smem] * scalars + [vmem] * (len(inputs) - scalars),
        out_specs=vmem if single else [vmem] * len(outs),
        scratch_shapes=list(scratch),
    )(*inputs)


def struct(shape, dtype=jnp.bfloat16):
    return jax.ShapeDtypeStruct(shape, dtype)


def spread(value, axis):
    return [value] + [shift(value, axis, k) for k in (1, 2, 3)]


def on_device(
    tokens, norm_gain_vector, query_weight, key_weight, value_weight, output_weight,
    prefix_cache, lengths, groups, deal_slot, owners,
):
    dp = lax.axis_index("dp")
    m = lax.axis_index("mp")
    y, zh, x, c = dp // 16, (dp // 4) % 4, dp % 4, m % 2
    pos = jnp.stack([y, zh, x, c, m]).astype(jnp.int32)

    by_head = jnp.stack(
        [
            jnp.concatenate(
                [w[:, 96 * h : 96 * h + 96] for w in (query_weight, key_weight, value_weight)], axis=1
            )
            for h in range(4)
        ]
    )
    block = prefix_cache[0]
    prefix_by_head = jnp.stack(
        [
            jnp.concatenate([block[:, 0, 96 * h : 96 * h + 96], block[:, 1, 96 * h : 96 * h + 96]], axis=1)
            for h in range(4)
        ]
    )

    def head_exchange(stacked):
        got = []
        for k in range(4):
            piece = lax.dynamic_index_in_dim(stacked, (y + k) % 4, 0, keepdims=False)
            got.append(piece if k == 0 else shift(piece, "y", k))
        return jnp.concatenate(got, axis=1)

    weight_rows = head_exchange(by_head)
    weight_z = jnp.stack(spread(weight_rows, "zh"))
    weight_pieces = spread(weight_z, "x")

    own = lax.dynamic_index_in_dim(tokens, c, 1, keepdims=False).astype(jnp.float32)
    scale = lax.rsqrt(jnp.mean(own * own, axis=-1, keepdims=True) + 1e-05)
    normed = (own * scale * norm_gain_vector).astype(jnp.bfloat16)
    extras = jnp.stack([deal_slot // 64, deal_slot % 64, lengths, groups], axis=1).astype(jnp.bfloat16)
    extras = jnp.pad(extras, ((0, 0), (0, 124)))
    sent = jnp.concatenate([normed, extras], axis=1)
    own_rows = jnp.stack(spread(sent, "y"))
    other_rows = mp_xor(own_rows, 1)

    prefix_rows = head_exchange(prefix_by_head)
    prefix_z = jnp.stack(spread(prefix_rows, "zh"))
    prefix_pieces = spread(prefix_z, "x")

    out_w = swap_y_mp(output_weight)
    out_z = jnp.stack(spread(out_w, "zh"))
    out_x = jnp.stack(spread(out_z, "x"))
    out_pieces = spread(out_x, "y")

    cosine, sine = rope_tables()
    queries, keyed, valued, info, send = call(
        qkv_kernel,
        [struct((512, 96)), struct((512, 96)), struct((512, 96)), struct((256, 128), jnp.float32), struct((64, 1664))],
        [pos, own_rows, other_rows, *weight_pieces, jnp.asarray(cosine), jnp.asarray(sine)],
        scratch=[pltpu.VMEM((4, 4, 48, 1152), jnp.bfloat16)],
        scalars=1,
    )
    received = lax.all_to_all(send, "dp", split_axis=0, concat_axis=0, tiled=True)

    r4 = jnp.arange(4, dtype=jnp.int32)
    source = (
        ((y - r4) % 4)[:, None, None] * 16 + ((x - r4) % 4)[None, :, None] + ((zh - r4) % 4)[None, None, :] * 4
    ).reshape(64)
    block_group = jnp.sum(
        jnp.where(owners[None, :] == source[:, None], (jnp.arange(64, dtype=jnp.int32) // 16)[None, :], 0), axis=1
    )
    key_group = jnp.broadcast_to(block_group.astype(jnp.float32)[:, None], (64, 64)).reshape(4, 1024)

    attended = call(
        attend_kernel,
        struct((512, 96)),
        [queries, keyed, valued, info, key_group, *prefix_pieces],
        scratch=[pltpu.VMEM((4, 256, 1024), jnp.float32)],
    )
    attended = attended.reshape(2, 4, 64, 96)
    back = [attended[:, 0]] + [shift(attended[:, k], "y", -k) for k in (1, 2, 3)]
    heads = []
    for h in range(4):
        at = (h - y) % 4
        heads.append(
            jnp.where(at < 2, jnp.where(at == 0, back[0], back[1]), jnp.where(at == 2, back[2], back[3]))
        )
    home = jnp.concatenate(heads, axis=2)
    home_all = [home] + [mp_xor(home, k) for k in (1, 2, 3)]

    out_weight = call(order_kernel, struct((4, 4, 4, 48, 384)), [pos, *out_pieces], scalars=1)
    hidden = call(
        out_kernel, struct((64, 1536)), [pos, *home_all, out_weight, lengths[:, None]], scalars=1
    ).reshape(64, 2, 768)
    suffix_cache = call(unpack_kernel, struct((64, 1536)), [received]).reshape(64, 2, 2, 384)
    return hidden, suffix_cache


def solution(mesh):
    in_specs = (
        P("dp", None, None),
        P(),
        P("dp", "mp"),
        P("dp", "mp"),
        P("dp", "mp"),
        P("dp", "mp"),
        P("dp", None, None, "mp"),
        P("dp"),
        P("dp"),
        P("dp"),
        P(),
    )
    out_specs = (P("dp", None, "mp"), P("dp", None, None, "mp"))
    return jax.shard_map(on_device, mesh=mesh, in_specs=in_specs, out_specs=out_specs, check_vma=False)
```

```python
import math

import jax
import jax.numpy as jnp
import numpy as np
from jax import lax
from jax.experimental import pallas as pl
from jax.experimental.pallas import tpu as pltpu
from jax.sharding import PartitionSpec as P


HD = 96
PREFIX = 1024
NEG = -1e30


def dp_shift(axis, amount):
    stride = {"y": 16, "zh": 4, "x": 1}[axis]
    perm = []
    for i in range(64):
        at = (i // stride) % 4
        perm.append((i, i + (((at + amount) % 4) - at) * stride))
    return perm


def shift(value, axis, amount):
    return lax.ppermute(value, "dp", dp_shift(axis, amount))


def mp_xor(value, mask):
    return lax.ppermute(value, "mp", [(i, i ^ mask) for i in range(4)])


def swap_y_mp(value):
    perm = []
    for i in range(64):
        y, rest = divmod(i, 16)
        for m in range(4):
            perm.append((i * 4 + m, (m * 16 + rest) * 4 + y))
    return lax.ppermute(value, ("dp", "mp"), perm)


def dot_nt(a, b):
    return lax.dot_general(a, b, (((1,), (1,)), ((), ())), preferred_element_type=jnp.float32)


def dot_tn(a, b):
    return lax.dot_general(a, b, (((0,), (0,)), ((), ())), preferred_element_type=jnp.float32)


def rope_tables():
    position = (PREFIX + np.arange(2)).astype(np.float32)
    frequency = np.float32(10000.0) ** (-np.arange(HD // 2).astype(np.float32) * np.float32(2.0) / np.float32(HD))
    angles = position[:, None] * frequency.astype(np.float32)[None, :]
    angles = np.concatenate([angles, angles], axis=-1).astype(np.float32)
    return np.cos(angles).astype(np.float32), np.sin(angles).astype(np.float32)


def qkv_kernel(
    pos_ref, own_ref, oth_ref, w0, w1, w2, w3, cos_ref, sin_ref,
    q_out, k_out, v_out, info_out, send_out, wsc,
):
    y, zh, x, c = pos_ref[0], pos_ref[1], pos_ref[2], pos_ref[3]
    for kx, piece in enumerate((w0, w1, w2, w3)):
        xa = (x - kx) & 3
        for kz in range(4):
            wsc[(zh - kz) & 3, xa] = piece[kz]
    accs = [None, None]
    for ky in range(4):
        ya = (y - ky) & 3
        lanes = pl.ds(pl.multiple_of(ya * 768, 128), 768)
        rhs = wsc[:, :, :, 288 * ky : 288 * ky + 288].reshape(768, 288)
        for i, ref in enumerate((own_ref, oth_ref)):
            part = jnp.dot(
                ref[:, :, lanes].reshape(256, 768), rhs, preferred_element_type=jnp.float32
            )
            accs[i] = part if accs[i] is None else accs[i] + part
    first = c == 0
    slots = (jnp.where(first, accs[0], accs[1]), jnp.where(first, accs[1], accs[0]))

    def rotate(values, t):
        turned = jnp.concatenate([-values[:, 48:], values[:, :48]], axis=1)
        return (values * cos_ref[t : t + 1, :] + turned * sin_ref[t : t + 1, :]).astype(jnp.bfloat16)

    info = own_ref[:, :, 3072:3200].reshape(256, 128).astype(jnp.float32)
    info_out[...] = info
    live = info[:, 2:3] > 1.5
    parts = []
    for t in range(2):
        rows = pl.ds(256 * t, 256)
        q_out[rows, :] = rotate(slots[t][:, :96], t)
        keyed = rotate(slots[t][:, 96:192], t)
        valued = slots[t][:, 192:288].astype(jnp.bfloat16)
        k_out[rows, :] = keyed
        v_out[rows, :] = valued
        if t == 1:
            keyed = jnp.where(live, keyed.astype(jnp.float32), 0.0).astype(jnp.bfloat16)
            valued = jnp.where(live, valued.astype(jnp.float32), 0.0).astype(jnp.bfloat16)
        parts += [keyed, valued]
    packed = jnp.concatenate(parts, axis=1)
    dest_iota = lax.broadcasted_iota(jnp.int32, (64, 64), 1).astype(jnp.float32)
    lane_iota = lax.broadcasted_iota(jnp.int32, (64, 128), 1)
    extras = jnp.zeros((64, 128), jnp.float32)
    for ky in range(4):
        block = info[64 * ky : 64 * ky + 64]
        pick = jnp.where(block[:, 0:1] == dest_iota, 1.0, 0.0).astype(jnp.bfloat16)
        moved = dot_tn(pick, packed[64 * ky : 64 * ky + 64])
        send_out[:, 384 * ky : 384 * ky + 384] = moved.astype(jnp.bfloat16)
        slot = jnp.where(lane_iota == ky, block[:, 1:2], 0.0).astype(jnp.bfloat16)
        extras = extras + dot_tn(pick, slot)
    send_out[:, 1536:1664] = extras.astype(jnp.bfloat16)


def attend_kernel(q_ref, k_ref, v_ref, info_ref, kg_ref, p0, p1, p2, p3, out_ref, s_ref, keys_ref, values_ref):
    factor = math.log2(math.e) / math.sqrt(HD)
    for ky in range(4):
        for kx, piece in enumerate((p0, p1, p2, p3)):
            rows = pl.ds(256 * kx, 256)
            keys_ref[ky, rows, :] = piece[:, :, 192 * ky : 192 * ky + 96].reshape(256, 96)
            values_ref[ky, rows, :] = piece[:, :, 192 * ky + 96 : 192 * ky + 192].reshape(256, 96)
    group = info_ref[:, 3:4]
    live = info_ref[:, 2:3] > 1.5

    def one_slot(t, carry):
        rows = pl.ds(pl.multiple_of(256 * t, 256), 256)
        queries = q_ref[rows, :]
        wide = queries.astype(jnp.float32)
        first = jnp.sum(wide * k_ref[0:256, :].astype(jnp.float32), axis=1, keepdims=True)
        second = jnp.sum(wide * k_ref[256:512, :].astype(jnp.float32), axis=1, keepdims=True)
        second = jnp.where(jnp.logical_and(live, t == 1), second, NEG)

        def score(ky, top):
            scores = dot_nt(queries, keys_ref[ky])
            scores = jnp.where(group == kg_ref[pl.ds(ky, 1), :], scores, NEG)
            s_ref[ky] = scores
            return jnp.maximum(top, jnp.max(scores, axis=1, keepdims=True))

        top = lax.fori_loop(0, 4, score, jnp.maximum(first, second))
        total = jnp.zeros((256, 1), jnp.float32)
        acc = jnp.zeros((256, 96), jnp.float32)
        for i, value in enumerate((first, second)):
            weight = jnp.exp2((value - top) * factor)
            total = total + weight
            values = v_ref[256 * i : 256 * i + 256, :].astype(jnp.float32)
            acc = acc + weight.astype(jnp.bfloat16).astype(jnp.float32) * values

        def gather(ky, state):
            total, acc = state
            weights = jnp.exp2((s_ref[ky] - top) * factor)
            total = total + jnp.sum(weights, axis=1, keepdims=True)
            acc = acc + jnp.dot(
                weights.astype(jnp.bfloat16), values_ref[ky], preferred_element_type=jnp.float32
            )
            return total, acc

        total, acc = lax.fori_loop(0, 4, gather, (total, acc))
        out_ref[rows, :] = (acc / total).astype(jnp.bfloat16)
        return carry

    lax.fori_loop(0, 2, one_slot, 0)


def order_kernel(pos_ref, w0, w1, w2, w3, out_ref):
    y, zh, x = pos_ref[0], pos_ref[1], pos_ref[2]
    for ky, piece in enumerate((w0, w1, w2, w3)):
        for kx in range(4):
            for kz in range(4):
                out_ref[(y - ky) & 3, (zh - kz) & 3, (x - kx) & 3] = piece[kx, kz]


def out_kernel(pos_ref, a0, a1, a2, a3, w_ref, len_ref, out_ref):
    m = pos_ref[4]
    acc = None
    for k, block in enumerate((a0, a1, a2, a3)):
        weight = w_ref[m ^ k].reshape(768, 384)
        part = dot_nt(block[...].reshape(128, 384), weight)
        acc = part if acc is None else acc + part
    out_ref[:, 0:768] = acc[0:64].astype(jnp.bfloat16)
    out_ref[:, 768:1536] = jnp.where(len_ref[...] > 1, acc[64:128], 0.0).astype(jnp.bfloat16)


def unpack_kernel(recv_ref, out_ref):
    slot_iota = lax.broadcasted_iota(jnp.int32, (64, 64), 1).astype(jnp.float32)
    for head in range(4):
        rows = pl.ds(16 * head, 16)
        data = jnp.concatenate(
            [recv_ref[rows, 384 * ky : 384 * ky + 384] for ky in range(4)], axis=0
        )
        tail = recv_ref[rows, 1536:1664].astype(jnp.float32)
        slots = jnp.concatenate([tail[:, ky : ky + 1] for ky in range(4)], axis=0)
        pick = jnp.where(slots == slot_iota, 1.0, 0.0).astype(jnp.bfloat16)
        moved = dot_tn(pick, data).astype(jnp.bfloat16)
        for part in range(4):
            out_ref[:, 384 * part + 96 * head : 384 * part + 96 * head + 96] = moved[
                :, 96 * part : 96 * part + 96
            ]


def call(kernel, outs, inputs, scratch=(), scalars=0):
    vmem = pl.BlockSpec(memory_space=pltpu.VMEM)
    smem = pl.BlockSpec(memory_space=pltpu.SMEM)
    single = not isinstance(outs, (list, tuple))
    return pl.pallas_call(
        kernel,
        out_shape=outs,
        in_specs=[smem] * scalars + [vmem] * (len(inputs) - scalars),
        out_specs=vmem if single else [vmem] * len(outs),
        scratch_shapes=list(scratch),
    )(*inputs)


def struct(shape, dtype=jnp.bfloat16):
    return jax.ShapeDtypeStruct(shape, dtype)


def spread(value, axis):
    return [value] + [shift(value, axis, k) for k in (1, 2, 3)]


def on_device(
    tokens, norm_gain_vector, query_weight, key_weight, value_weight, output_weight,
    prefix_cache, lengths, groups, deal_slot, owners,
):
    dp = lax.axis_index("dp")
    m = lax.axis_index("mp")
    y, zh, x, c = dp // 16, (dp // 4) % 4, dp % 4, m % 2
    pos = jnp.stack([y, zh, x, c, m]).astype(jnp.int32)

    by_head = jnp.stack(
        [
            jnp.concatenate(
                [w[:, 96 * h : 96 * h + 96] for w in (query_weight, key_weight, value_weight)], axis=1
            )
            for h in range(4)
        ]
    )
    block = prefix_cache[0]
    prefix_by_head = jnp.stack(
        [
            jnp.concatenate([block[:, 0, 96 * h : 96 * h + 96], block[:, 1, 96 * h : 96 * h + 96]], axis=1)
            for h in range(4)
        ]
    )

    def head_exchange(stacked):
        got = []
        for k in range(4):
            piece = lax.dynamic_index_in_dim(stacked, (y + k) % 4, 0, keepdims=False)
            got.append(piece if k == 0 else shift(piece, "y", k))
        return jnp.concatenate(got, axis=1)

    weight_rows = head_exchange(by_head)
    weight_z = jnp.stack(spread(weight_rows, "zh"))
    weight_pieces = spread(weight_z, "x")

    own = lax.dynamic_index_in_dim(tokens, c, 1, keepdims=False).astype(jnp.float32)
    scale = lax.rsqrt(jnp.mean(own * own, axis=-1, keepdims=True) + 1e-05)
    normed = (own * scale * norm_gain_vector).astype(jnp.bfloat16)
    extras = jnp.stack([deal_slot // 64, deal_slot % 64, lengths, groups], axis=1).astype(jnp.bfloat16)
    extras = jnp.pad(extras, ((0, 0), (0, 124)))
    sent = jnp.concatenate([normed, extras], axis=1)
    own_rows = jnp.stack(spread(sent, "y"))
    other_rows = mp_xor(own_rows, 1)

    prefix_rows = head_exchange(prefix_by_head)
    prefix_z = jnp.stack(spread(prefix_rows, "zh"))
    prefix_pieces = spread(prefix_z, "x")

    out_w = swap_y_mp(output_weight)
    out_z = jnp.stack(spread(out_w, "zh"))
    out_x = jnp.stack(spread(out_z, "x"))
    out_pieces = spread(out_x, "y")

    cosine, sine = rope_tables()
    queries, keyed, valued, info, send = call(
        qkv_kernel,
        [struct((512, 96)), struct((512, 96)), struct((512, 96)), struct((256, 128), jnp.float32), struct((64, 1664))],
        [pos, own_rows, other_rows, *weight_pieces, jnp.asarray(cosine), jnp.asarray(sine)],
        scratch=[pltpu.VMEM((4, 4, 48, 1152), jnp.bfloat16)],
        scalars=1,
    )
    received = lax.all_to_all(send, "dp", split_axis=0, concat_axis=0, tiled=True)

    r4 = jnp.arange(4, dtype=jnp.int32)
    source = (
        ((y - r4) % 4)[:, None, None] * 16 + ((x - r4) % 4)[None, :, None] + ((zh - r4) % 4)[None, None, :] * 4
    ).reshape(64)
    block_group = jnp.sum(
        jnp.where(owners[None, :] == source[:, None], (jnp.arange(64, dtype=jnp.int32) // 16)[None, :], 0), axis=1
    )
    key_group = jnp.broadcast_to(block_group.astype(jnp.float32)[:, None], (64, 64)).reshape(4, 1024)

    attended = call(
        attend_kernel,
        struct((512, 96)),
        [queries, keyed, valued, info, key_group, *prefix_pieces],
        scratch=[
            pltpu.VMEM((4, 256, 1024), jnp.float32),
            pltpu.VMEM((4, 1024, 96), jnp.bfloat16),
            pltpu.VMEM((4, 1024, 96), jnp.bfloat16),
        ],
    )
    attended = attended.reshape(2, 4, 64, 96)
    back = [attended[:, 0]] + [shift(attended[:, k], "y", -k) for k in (1, 2, 3)]
    heads = []
    for h in range(4):
        at = (h - y) % 4
        heads.append(
            jnp.where(at < 2, jnp.where(at == 0, back[0], back[1]), jnp.where(at == 2, back[2], back[3]))
        )
    home = jnp.concatenate(heads, axis=2)
    home_all = [home] + [mp_xor(home, k) for k in (1, 2, 3)]

    out_weight = call(order_kernel, struct((4, 4, 4, 48, 384)), [pos, *out_pieces], scalars=1)
    hidden = call(
        out_kernel, struct((64, 1536)), [pos, *home_all, out_weight, lengths[:, None]], scalars=1
    ).reshape(64, 2, 768)
    suffix_cache = call(unpack_kernel, struct((64, 1536)), [received]).reshape(64, 2, 2, 384)
    return hidden, suffix_cache


def solution(mesh):
    in_specs = (
        P("dp", None, None),
        P(),
        P("dp", "mp"),
        P("dp", "mp"),
        P("dp", "mp"),
        P("dp", "mp"),
        P("dp", None, None, "mp"),
        P("dp"),
        P("dp"),
        P("dp"),
        P(),
    )
    out_specs = (P("dp", None, "mp"), P("dp", None, None, "mp"))
    return jax.shard_map(on_device, mesh=mesh, in_specs=in_specs, out_specs=out_specs, check_vma=False)
```

```python
import math

import jax
import jax.numpy as jnp
import numpy as np
from jax import lax
from jax.experimental import pallas as pl
from jax.experimental.pallas import tpu as pltpu
from jax.sharding import PartitionSpec as P


HD = 96
PREFIX = 1024
NEG = -1e30


def place(dp, m):
    return dp // 16, (dp // 4) % 4, dp % 4, m // 2, m % 2


def index_of(y, zh, x, zl, core):
    return ((y % 4) * 16 + (zh % 4) * 4 + x % 4) * 4 + zl * 2 + core


def move(value, where):
    perm = []
    for dp in range(64):
        for m in range(4):
            perm.append((dp * 4 + m, index_of(*where(*place(dp, m)))))
    return lax.ppermute(value, ("dp", "mp"), perm)


def shift(value, axis, k):
    step = {"y": (k, 0, 0), "zh": (0, k, 0), "x": (0, 0, k)}[axis]
    return move(value, lambda y, zh, x, zl, core: (y + step[0], zh + step[1], x + step[2], zl, core))


def mp_xor(value, mask):
    return move(value, lambda y, zh, x, zl, core: (y, zh, x, zl ^ (mask // 2), core ^ (mask % 2)))


def swap_y_mp(value):
    return move(value, lambda y, zh, x, zl, core: (2 * zl + core, zh, x, y // 2, y % 2))


def next_chip(value):
    return move(value, lambda y, zh, x, zl, core: (y, zh + 1 if zl else zh - 1, x, 1 - zl, core))


def to_pair(value, side):
    return move(value, lambda y, zh, x, zl, core: (y, zh + side if zl else zh - side, x, zl, core))


def dot_nt(a, b):
    return lax.dot_general(a, b, (((1,), (1,)), ((), ())), preferred_element_type=jnp.float32)


def dot_tn(a, b):
    return lax.dot_general(a, b, (((0,), (0,)), ((), ())), preferred_element_type=jnp.float32)


def rope_tables():
    position = (PREFIX + np.arange(2)).astype(np.float32)
    frequency = np.float32(10000.0) ** (-np.arange(HD // 2).astype(np.float32) * np.float32(2.0) / np.float32(HD))
    angles = position[:, None] * frequency.astype(np.float32)[None, :]
    angles = np.concatenate([angles, angles], axis=-1).astype(np.float32)
    return np.cos(angles).astype(np.float32), np.sin(angles).astype(np.float32)


def qkv_kernel(
    pos_ref, own_ref, oth_ref, w0, w1, w2, w3, cos_ref, sin_ref,
    q_out, k_out, v_out, info_out, send_out, wsc,
):
    y, zh, x, c = pos_ref[0], pos_ref[1], pos_ref[2], pos_ref[3]
    for kx, piece in enumerate((w0, w1, w2, w3)):
        xa = (x - kx) & 3
        for kz in range(4):
            for ky in range(4):
                wsc[(y - ky) & 3, (zh - kz) & 3, xa] = piece[ky, :, 288 * kz : 288 * kz + 288]
    rhs = wsc[...].reshape(3072, 288)
    accs = [
        jnp.dot(ref[:, :, 0:3072].reshape(256, 3072), rhs, preferred_element_type=jnp.float32)
        for ref in (own_ref, oth_ref)
    ]
    first = c == 0
    slots = (jnp.where(first, accs[0], accs[1]), jnp.where(first, accs[1], accs[0]))

    def rotate(values, t):
        turned = jnp.concatenate([-values[:, 48:], values[:, :48]], axis=1)
        return (values * cos_ref[t : t + 1, :] + turned * sin_ref[t : t + 1, :]).astype(jnp.bfloat16)

    info = own_ref[:, :, 3072:3200].reshape(256, 128).astype(jnp.float32)
    info_out[...] = info
    live = info[:, 2:3] > 1.5
    parts = []
    for t in range(2):
        rows = pl.ds(256 * t, 256)
        q_out[rows, :] = rotate(slots[t][:, :96], t)
        keyed = rotate(slots[t][:, 96:192], t)
        valued = slots[t][:, 192:288].astype(jnp.bfloat16)
        k_out[rows, :] = keyed
        v_out[rows, :] = valued
        if t == 1:
            keyed = jnp.where(live, keyed.astype(jnp.float32), 0.0).astype(jnp.bfloat16)
            valued = jnp.where(live, valued.astype(jnp.float32), 0.0).astype(jnp.bfloat16)
        parts += [keyed, valued]
    packed = jnp.concatenate(parts, axis=1)
    dest_iota = lax.broadcasted_iota(jnp.int32, (64, 64), 1).astype(jnp.float32)
    lane_iota = lax.broadcasted_iota(jnp.int32, (64, 128), 1)
    extras = jnp.zeros((64, 128), jnp.float32)
    for ky in range(4):
        block = info[64 * ky : 64 * ky + 64]
        pick = jnp.where(block[:, 0:1] == dest_iota, 1.0, 0.0).astype(jnp.bfloat16)
        moved = dot_tn(pick, packed[64 * ky : 64 * ky + 64])
        send_out[:, 384 * ky : 384 * ky + 384] = moved.astype(jnp.bfloat16)
        slot = jnp.where(lane_iota == ky, block[:, 1:2], 0.0).astype(jnp.bfloat16)
        extras = extras + dot_tn(pick, slot)
    send_out[:, 1536:1664] = extras.astype(jnp.bfloat16)


def attend_kernel(q_ref, k_ref, v_ref, info_ref, kg_ref, p0, p1, p2, p3, out_ref, s_ref, keys_ref, values_ref):
    factor = math.log2(math.e) / math.sqrt(HD)
    for kz in range(4):
        for ky, piece in enumerate((p0, p1, p2, p3)):
            for half in range(2):
                rows = pl.ds(256 * ky + 128 * half, 128)
                lane = 384 * kz + 192 * half
                keys_ref[kz, rows, :] = piece[:, :, lane : lane + 96].reshape(128, 96)
                values_ref[kz, rows, :] = piece[:, :, lane + 96 : lane + 192].reshape(128, 96)
    group = info_ref[:, 3:4]
    live = info_ref[:, 2:3] > 1.5

    def one_slot(t):
        rows = pl.ds(256 * t, 256)
        queries = q_ref[rows, :]
        wide = queries.astype(jnp.float32)
        first = jnp.sum(wide * k_ref[0:256, :].astype(jnp.float32), axis=1, keepdims=True)
        second = jnp.sum(wide * k_ref[256:512, :].astype(jnp.float32), axis=1, keepdims=True)
        second = jnp.where(live, second, NEG) if t == 1 else jnp.full_like(second, NEG)

        def score(ky, top):
            scores = dot_nt(queries, keys_ref[ky])
            scores = jnp.where(group == kg_ref[ky : ky + 1, :], scores, NEG)
            s_ref[ky] = scores
            return jnp.maximum(top, jnp.max(scores, axis=1, keepdims=True))

        top = jnp.maximum(first, second)
        for kz in range(4):
            top = score(kz, top)
        total = jnp.zeros((256, 1), jnp.float32)
        acc = jnp.zeros((256, 96), jnp.float32)
        for i, value in enumerate((first, second)):
            weight = jnp.exp2((value - top) * factor)
            total = total + weight
            values = v_ref[256 * i : 256 * i + 256, :].astype(jnp.float32)
            acc = acc + weight.astype(jnp.bfloat16).astype(jnp.float32) * values

        def gather(ky, state):
            total, acc = state
            weights = jnp.exp2((s_ref[ky] - top) * factor)
            total = total + jnp.sum(weights, axis=1, keepdims=True)
            acc = acc + jnp.dot(
                weights.astype(jnp.bfloat16), values_ref[ky], preferred_element_type=jnp.float32
            )
            return total, acc

        for kz in range(4):
            total, acc = gather(kz, (total, acc))
        out_ref[rows, :] = (acc / total).astype(jnp.bfloat16)

    for t in range(2):
        one_slot(t)


def order_kernel(pos_ref, w0, w1, w2, w3, out_ref):
    y, zh, x = pos_ref[0], pos_ref[1], pos_ref[2]
    for ky, piece in enumerate((w0, w1, w2, w3)):
        for kx in range(4):
            for kz in range(4):
                out_ref[(y - ky) & 3, (zh - kz) & 3, (x - kx) & 3] = piece[kx, :, 384 * kz : 384 * kz + 384]


def out_kernel(pos_ref, a0, a1, a2, a3, w_ref, len_ref, out_ref):
    m = pos_ref[4]
    acc = None
    for k, block in enumerate((a0, a1, a2, a3)):
        weight = w_ref[m ^ k].reshape(768, 384)
        part = dot_nt(block[...].reshape(128, 384), weight)
        acc = part if acc is None else acc + part
    out_ref[:, 0:768] = acc[0:64].astype(jnp.bfloat16)
    out_ref[:, 768:1536] = jnp.where(len_ref[...] > 1, acc[64:128], 0.0).astype(jnp.bfloat16)


def unpack_kernel(recv_ref, out_ref):
    slot_iota = lax.broadcasted_iota(jnp.int32, (256, 64), 1).astype(jnp.float32)
    source_head = (lax.broadcasted_iota(jnp.int32, (256, 1), 0) // 4) % 4
    data = jnp.concatenate([recv_ref[:, 384 * k : 384 * k + 384] for k in range(4)], axis=0)
    tail = recv_ref[:, 1536:1664].astype(jnp.float32)
    slots = jnp.concatenate([tail[:, k : k + 1] for k in range(4)], axis=0)
    for head in range(4):
        own = jnp.where(source_head == head, slots, -1.0)
        pick = jnp.where(own == slot_iota, 1.0, 0.0).astype(jnp.bfloat16)
        moved = dot_tn(pick, data).astype(jnp.bfloat16)
        for part in range(4):
            out_ref[:, 384 * part + 96 * head : 384 * part + 96 * head + 96] = moved[
                :, 96 * part : 96 * part + 96
            ]


def call(kernel, outs, inputs, scratch=(), scalars=0):
    vmem = pl.BlockSpec(memory_space=pltpu.VMEM)
    smem = pl.BlockSpec(memory_space=pltpu.SMEM)
    single = not isinstance(outs, (list, tuple))
    return pl.pallas_call(
        kernel,
        out_shape=outs,
        in_specs=[smem] * scalars + [vmem] * (len(inputs) - scalars),
        out_specs=vmem if single else [vmem] * len(outs),
        scratch_shapes=list(scratch),
    )(*inputs)


def struct(shape, dtype=jnp.bfloat16):
    return jax.ShapeDtypeStruct(shape, dtype)


def spread(value, axis):
    return [value] + [shift(value, axis, k) for k in (1, 2, 3)]


def on_device(
    tokens, norm_gain_vector, query_weight, key_weight, value_weight, output_weight,
    prefix_cache, lengths, groups, deal_slot, owners,
):
    dp = lax.axis_index("dp")
    m = lax.axis_index("mp")
    y, zh, x, c = dp // 16, (dp // 4) % 4, dp % 4, m % 2
    pos = jnp.stack([y, zh, x, c, m]).astype(jnp.int32)

    zl = m // 2
    block = prefix_cache[0]
    blank = jnp.zeros((48, 96), jnp.bfloat16)
    by_head = []
    for h in range(4):
        cols = slice(96 * h, 96 * h + 96)
        projections = [w[:, cols] for w in (query_weight, key_weight, value_weight)]
        pairs = [block[r : r + 32, kind, cols] for r in (0, 32) for kind in (0, 1)]
        by_head.append(
            jnp.concatenate(
                [jnp.concatenate([*projections, blank], axis=1), jnp.concatenate(pairs, axis=1)], axis=0
            )
        )
    by_head = jnp.stack(by_head)
    got = []
    for k in range(4):
        piece = lax.dynamic_index_in_dim(by_head, (zh + k) % 4, 0, keepdims=False)
        piece = jnp.concatenate([piece, output_weight], axis=0)
        got.append(piece if k == 0 else shift(piece, "zh", k))
    weight_rows = jnp.concatenate([g[0:48, 0:288] for g in got], axis=1)
    prefix_rows = jnp.concatenate([g[48:80] for g in got], axis=1)
    out_rows = jnp.concatenate([g[80:128] for g in got], axis=1)

    own = lax.dynamic_index_in_dim(tokens, c, 1, keepdims=False).astype(jnp.float32)
    scale = lax.rsqrt(jnp.mean(own * own, axis=-1, keepdims=True) + 1e-05)
    normed = (own * scale * norm_gain_vector).astype(jnp.bfloat16)
    extras = jnp.stack([deal_slot // 64, deal_slot % 64, lengths, groups], axis=1).astype(jnp.bfloat16)
    extras = jnp.pad(extras, ((0, 0), (0, 124)))
    sent = jnp.concatenate([normed, extras], axis=1)
    outer = next_chip(sent)
    inner = mp_xor(outer, 2)
    far = next_chip(inner)
    own_rows = jnp.stack([sent, outer, inner, far])
    other_rows = mp_xor(own_rows, 1)

    weight_pieces = spread(jnp.stack(spread(weight_rows, "y")), "x")
    both = jnp.concatenate([prefix_rows, swap_y_mp(out_rows)], axis=0)
    both_x = spread(both, "x")
    prefix_pieces = spread(jnp.stack([b[0:32] for b in both_x]), "y")
    out_pieces = spread(jnp.stack([b[32:80] for b in both_x]), "y")

    cosine, sine = rope_tables()
    queries, keyed, valued, info, send = call(
        qkv_kernel,
        [struct((512, 96)), struct((512, 96)), struct((512, 96)), struct((256, 128), jnp.float32), struct((64, 1664))],
        [pos, own_rows, other_rows, *weight_pieces, jnp.asarray(cosine), jnp.asarray(sine)],
        scratch=[pltpu.VMEM((4, 4, 4, 48, 288), jnp.bfloat16)],
        scalars=1,
    )
    received = lax.all_to_all(send, "dp", split_axis=0, concat_axis=0, tiled=True)

    r4 = jnp.arange(4, dtype=jnp.int32)
    source = (
        ((zh - r4) % 4)[:, None, None] * 4 + ((y - r4) % 4)[None, :, None] * 16 + ((x - r4) % 4)[None, None, :]
    ).reshape(64)
    block_group = jnp.sum(
        jnp.where(owners[None, :] == source[:, None], (jnp.arange(64, dtype=jnp.int32) // 16)[None, :], 0), axis=1
    )
    key_group = jnp.broadcast_to(
        block_group.astype(jnp.float32).reshape(4, 4, 1, 4, 1), (4, 4, 2, 4, 32)
    ).reshape(4, 1024)

    attended = call(
        attend_kernel,
        struct((512, 96)),
        [queries, keyed, valued, info, key_group, *prefix_pieces],
        scratch=[
            pltpu.VMEM((4, 256, 1024), jnp.float32),
            pltpu.VMEM((4, 1024, 96), jnp.bfloat16),
            pltpu.VMEM((4, 1024, 96), jnp.bfloat16),
        ],
    )
    attended = attended.reshape(2, 4, 64, 96)
    back = [attended[:, 0], to_pair(attended[:, 1], 1), to_pair(attended[:, 2], -1), to_pair(attended[:, 3], 2)]
    heads = []
    for h in range(4):
        at = jnp.where(zl == 0, h - zh, zh - h) % 4
        heads.append(
            jnp.where(at < 2, jnp.where(at == 0, back[0], back[1]), jnp.where(at == 2, back[3], back[2]))
        )
    home = jnp.concatenate(heads, axis=2)
    home_all = [home] + [mp_xor(home, k) for k in (1, 2, 3)]

    out_weight = call(order_kernel, struct((4, 4, 4, 48, 384)), [pos, *out_pieces], scalars=1)
    hidden = call(
        out_kernel, struct((64, 1536)), [pos, *home_all, out_weight, lengths[:, None]], scalars=1
    ).reshape(64, 2, 768)
    suffix_cache = call(unpack_kernel, struct((64, 1536)), [received]).reshape(64, 2, 2, 384)
    return hidden, suffix_cache


def solution(mesh):
    in_specs = (
        P("dp", None, None),
        P(),
        P("dp", "mp"),
        P("dp", "mp"),
        P("dp", "mp"),
        P("dp", "mp"),
        P("dp", None, None, "mp"),
        P("dp"),
        P("dp"),
        P("dp"),
        P(),
    )
    out_specs = (P("dp", None, "mp"), P("dp", None, None, "mp"))
    return jax.shard_map(on_device, mesh=mesh, in_specs=in_specs, out_specs=out_specs, check_vma=False)
```

```python
import math

import jax
import jax.numpy as jnp
import numpy as np
from jax import lax
from jax.experimental import pallas as pl
from jax.experimental.pallas import tpu as pltpu
from jax.sharding import PartitionSpec as P


HD = 96
PREFIX = 1024
NEG = -1e30


def place(dp, m):
    return dp // 16, (dp // 4) % 4, dp % 4, m // 2, m % 2


def index_of(y, zh, x, zl, core):
    return ((y % 4) * 16 + (zh % 4) * 4 + x % 4) * 4 + zl * 2 + core


def move(value, where):
    perm = []
    for dp in range(64):
        for m in range(4):
            perm.append((dp * 4 + m, index_of(*where(*place(dp, m)))))
    return lax.ppermute(value, ("dp", "mp"), perm)


def shift(value, axis, k):
    step = {"y": (k, 0, 0), "zh": (0, k, 0), "x": (0, 0, k)}[axis]
    return move(value, lambda y, zh, x, zl, core: (y + step[0], zh + step[1], x + step[2], zl, core))


def mp_xor(value, mask):
    return move(value, lambda y, zh, x, zl, core: (y, zh, x, zl ^ (mask // 2), core ^ (mask % 2)))


def swap_y_mp(value):
    return move(value, lambda y, zh, x, zl, core: (2 * zl + core, zh, x, y // 2, y % 2))


def next_chip(value):
    return move(value, lambda y, zh, x, zl, core: (y, zh + 1 if zl else zh - 1, x, 1 - zl, core))


def to_pair(value, side):
    return move(value, lambda y, zh, x, zl, core: (y, zh + side if zl else zh - side, x, zl, core))


def dot_nt(a, b):
    return lax.dot_general(a, b, (((1,), (1,)), ((), ())), preferred_element_type=jnp.float32)


def dot_tn(a, b):
    return lax.dot_general(a, b, (((0,), (0,)), ((), ())), preferred_element_type=jnp.float32)


def rope_tables():
    position = (PREFIX + np.arange(2)).astype(np.float32)
    frequency = np.float32(10000.0) ** (-np.arange(HD // 2).astype(np.float32) * np.float32(2.0) / np.float32(HD))
    angles = position[:, None] * frequency.astype(np.float32)[None, :]
    angles = np.concatenate([angles, angles], axis=-1).astype(np.float32)
    return np.cos(angles).astype(np.float32), np.sin(angles).astype(np.float32)


def qkv_kernel(
    pos_ref, own_ref, oth_ref, w0, w1, w2, w3, cos_ref, sin_ref,
    q_out, k_out, v_out, info_out, send_out, wsc,
):
    y, zh, x, c = pos_ref[0], pos_ref[1], pos_ref[2], pos_ref[3]
    for kx, piece in enumerate((w0, w1, w2, w3)):
        xa = (x - kx) & 3
        for kz in range(4):
            for ky in range(4):
                wsc[(y - ky) & 3, (zh - kz) & 3, xa] = piece[ky, :, 288 * kz : 288 * kz + 288]
    rhs = wsc[...].reshape(3072, 288)
    accs = [
        jnp.dot(ref[:, :, 0:3072].reshape(256, 3072), rhs, preferred_element_type=jnp.float32)
        for ref in (own_ref, oth_ref)
    ]
    first = c == 0
    slots = (jnp.where(first, accs[0], accs[1]), jnp.where(first, accs[1], accs[0]))

    def rotate(values, t):
        turned = jnp.concatenate([-values[:, 48:], values[:, :48]], axis=1)
        return (values * cos_ref[t : t + 1, :] + turned * sin_ref[t : t + 1, :]).astype(jnp.bfloat16)

    info = own_ref[:, :, 3072:3200].reshape(256, 128).astype(jnp.float32)
    info_out[...] = info
    live = info[:, 2:3] > 1.5
    parts = []
    for t in range(2):
        rows = pl.ds(256 * t, 256)
        q_out[rows, :] = rotate(slots[t][:, :96], t)
        keyed = rotate(slots[t][:, 96:192], t)
        valued = slots[t][:, 192:288].astype(jnp.bfloat16)
        k_out[rows, :] = keyed
        v_out[rows, :] = valued
        if t == 1:
            keyed = jnp.where(live, keyed.astype(jnp.float32), 0.0).astype(jnp.bfloat16)
            valued = jnp.where(live, valued.astype(jnp.float32), 0.0).astype(jnp.bfloat16)
        parts += [keyed, valued]
    packed = jnp.concatenate(parts, axis=1)
    dest_iota = lax.broadcasted_iota(jnp.int32, (64, 64), 1).astype(jnp.float32)
    lane_iota = lax.broadcasted_iota(jnp.int32, (64, 128), 1)
    extras = jnp.zeros((64, 128), jnp.float32)
    for ky in range(4):
        block = info[64 * ky : 64 * ky + 64]
        pick = jnp.where(block[:, 0:1] == dest_iota, 1.0, 0.0).astype(jnp.bfloat16)
        moved = dot_tn(pick, packed[64 * ky : 64 * ky + 64])
        send_out[:, 384 * ky : 384 * ky + 384] = moved.astype(jnp.bfloat16)
        slot = jnp.where(lane_iota == ky, block[:, 1:2], 0.0).astype(jnp.bfloat16)
        extras = extras + dot_tn(pick, slot)
    send_out[:, 1536:1664] = extras.astype(jnp.bfloat16)


def attend_kernel(q_ref, k_ref, v_ref, info_ref, kg_ref, p0, p1, p2, p3, out_ref, s_ref, keys_ref, values_ref):
    factor = math.log2(math.e) / math.sqrt(HD)
    for kz in range(4):
        for ky, piece in enumerate((p0, p1, p2, p3)):
            for half in range(2):
                rows = pl.ds(256 * ky + 128 * half, 128)
                lane = 384 * kz + 192 * half
                keys_ref[kz, rows, :] = piece[:, :, lane : lane + 96].reshape(128, 96)
                values_ref[kz, rows, :] = piece[:, :, lane + 96 : lane + 192].reshape(128, 96)
    group = info_ref[:, 3:4]
    live = info_ref[:, 2:3] > 1.5

    def one_slot(t):
        rows = pl.ds(256 * t, 256)
        queries = q_ref[rows, :]
        wide = queries.astype(jnp.float32)
        first = jnp.sum(wide * k_ref[0:256, :].astype(jnp.float32), axis=1, keepdims=True)
        second = jnp.sum(wide * k_ref[256:512, :].astype(jnp.float32), axis=1, keepdims=True)
        second = jnp.where(live, second, NEG) if t == 1 else jnp.full_like(second, NEG)

        def score(ky, top):
            scores = dot_nt(queries, keys_ref[ky])
            scores = jnp.where(group == kg_ref[ky : ky + 1, :], scores, NEG)
            s_ref[ky] = scores
            return jnp.maximum(top, jnp.max(scores, axis=1, keepdims=True))

        top = jnp.maximum(first, second)
        for kz in range(4):
            top = score(kz, top)
        total = jnp.zeros((256, 1), jnp.float32)
        acc = jnp.zeros((256, 96), jnp.float32)
        for i, value in enumerate((first, second)):
            weight = jnp.exp2((value - top) * factor)
            total = total + weight
            values = v_ref[256 * i : 256 * i + 256, :].astype(jnp.float32)
            acc = acc + weight.astype(jnp.bfloat16).astype(jnp.float32) * values

        def gather(ky, state):
            total, acc = state
            weights = jnp.exp2((s_ref[ky] - top) * factor)
            total = total + jnp.sum(weights, axis=1, keepdims=True)
            acc = acc + jnp.dot(
                weights.astype(jnp.bfloat16), values_ref[ky], preferred_element_type=jnp.float32
            )
            return total, acc

        for kz in range(4):
            total, acc = gather(kz, (total, acc))
        out_ref[rows, :] = (acc / total).astype(jnp.bfloat16)

    for t in range(2):
        one_slot(t)


def order_kernel(pos_ref, w0, w1, w2, w3, out_ref):
    y, zh, x = pos_ref[0], pos_ref[1], pos_ref[2]
    for ky, piece in enumerate((w0, w1, w2, w3)):
        for kx in range(4):
            for kz in range(4):
                out_ref[(y - ky) & 3, (zh - kz) & 3, (x - kx) & 3] = piece[kx, :, 384 * kz : 384 * kz + 384]


def out_kernel(pos_ref, a0, a1, a2, a3, w_ref, len_ref, out_ref):
    m = pos_ref[4]
    acc = None
    for k, block in enumerate((a0, a1, a2, a3)):
        weight = w_ref[m ^ k].reshape(768, 384)
        part = dot_nt(block[...].reshape(128, 384), weight)
        acc = part if acc is None else acc + part
    out_ref[:, 0:768] = acc[0:64].astype(jnp.bfloat16)
    out_ref[:, 768:1536] = jnp.where(len_ref[...] > 1, acc[64:128], 0.0).astype(jnp.bfloat16)


def unpack_kernel(recv_ref, out_ref):
    slot_iota = lax.broadcasted_iota(jnp.int32, (256, 64), 1).astype(jnp.float32)
    source_head = (lax.broadcasted_iota(jnp.int32, (256, 1), 0) // 4) % 4
    data = jnp.concatenate([recv_ref[:, 384 * k : 384 * k + 384] for k in range(4)], axis=0)
    tail = recv_ref[:, 1536:1664].astype(jnp.float32)
    slots = jnp.concatenate([tail[:, k : k + 1] for k in range(4)], axis=0)
    for head in range(4):
        own = jnp.where(source_head == head, slots, -1.0)
        pick = jnp.where(own == slot_iota, 1.0, 0.0).astype(jnp.bfloat16)
        moved = dot_tn(pick, data).astype(jnp.bfloat16)
        for part in range(4):
            out_ref[:, 384 * part + 96 * head : 384 * part + 96 * head + 96] = moved[
                :, 96 * part : 96 * part + 96
            ]


def call(kernel, outs, inputs, scratch=(), scalars=0):
    vmem = pl.BlockSpec(memory_space=pltpu.VMEM)
    smem = pl.BlockSpec(memory_space=pltpu.SMEM)
    single = not isinstance(outs, (list, tuple))
    return pl.pallas_call(
        kernel,
        out_shape=outs,
        in_specs=[smem] * scalars + [vmem] * (len(inputs) - scalars),
        out_specs=vmem if single else [vmem] * len(outs),
        scratch_shapes=list(scratch),
    )(*inputs)


def struct(shape, dtype=jnp.bfloat16):
    return jax.ShapeDtypeStruct(shape, dtype)


def spread(value, axis):
    return [value] + [shift(value, axis, k) for k in (1, 2, 3)]


def on_device(
    tokens, norm_gain_vector, query_weight, key_weight, value_weight, output_weight,
    prefix_cache, lengths, groups, deal_slot, owners,
):
    dp = lax.axis_index("dp")
    m = lax.axis_index("mp")
    y, zh, x, c = dp // 16, (dp // 4) % 4, dp % 4, m % 2
    pos = jnp.stack([y, zh, x, c, m]).astype(jnp.int32)

    zl = m // 2
    block = prefix_cache[0]
    blank = jnp.zeros((48, 96), jnp.bfloat16)
    by_head = []
    for h in range(4):
        cols = slice(96 * h, 96 * h + 96)
        projections = [w[:, cols] for w in (query_weight, key_weight, value_weight)]
        pairs = [block[r : r + 32, kind, cols] for r in (0, 32) for kind in (0, 1)]
        by_head.append(
            jnp.concatenate(
                [jnp.concatenate([*projections, blank], axis=1), jnp.concatenate(pairs, axis=1)], axis=0
            )
        )
    by_head = jnp.stack(by_head)
    got = []
    for k in range(4):
        piece = lax.dynamic_index_in_dim(by_head, (zh + k) % 4, 0, keepdims=False)
        piece = jnp.concatenate([piece, output_weight], axis=0)
        got.append(piece if k == 0 else shift(piece, "zh", k))
    weight_rows = jnp.concatenate([g[0:48, 0:288] for g in got], axis=1)
    prefix_rows = jnp.concatenate([g[48:80] for g in got], axis=1)
    out_rows = jnp.concatenate([g[80:128] for g in got], axis=1)

    own = lax.dynamic_index_in_dim(tokens, c, 1, keepdims=False).astype(jnp.float32)
    scale = lax.rsqrt(jnp.mean(own * own, axis=-1, keepdims=True) + 1e-05)
    normed = (own * scale * norm_gain_vector).astype(jnp.bfloat16)
    extras = jnp.stack([deal_slot // 64, deal_slot % 64, lengths, groups], axis=1).astype(jnp.bfloat16)
    extras = jnp.pad(extras, ((0, 0), (0, 124)))
    sent = jnp.concatenate([normed, extras], axis=1)
    outer = next_chip(sent)
    inner = mp_xor(outer, 2)
    far = next_chip(inner)
    own_rows = jnp.stack([sent, outer, inner, far])
    other_rows = mp_xor(own_rows, 1)

    weight_pieces = spread(jnp.stack(spread(weight_rows, "y")), "x")
    prefix_pieces = spread(jnp.stack(spread(prefix_rows, "x")), "y")
    out_pieces = spread(jnp.stack(spread(swap_y_mp(out_rows), "x")), "y")

    cosine, sine = rope_tables()
    queries, keyed, valued, info, send = call(
        qkv_kernel,
        [struct((512, 96)), struct((512, 96)), struct((512, 96)), struct((256, 128), jnp.float32), struct((64, 1664))],
        [pos, own_rows, other_rows, *weight_pieces, jnp.asarray(cosine), jnp.asarray(sine)],
        scratch=[pltpu.VMEM((4, 4, 4, 48, 288), jnp.bfloat16)],
        scalars=1,
    )
    received = lax.all_to_all(send, "dp", split_axis=0, concat_axis=0, tiled=True)

    r4 = jnp.arange(4, dtype=jnp.int32)
    source = (
        ((zh - r4) % 4)[:, None, None] * 4 + ((y - r4) % 4)[None, :, None] * 16 + ((x - r4) % 4)[None, None, :]
    ).reshape(64)
    block_group = jnp.sum(
        jnp.where(owners[None, :] == source[:, None], (jnp.arange(64, dtype=jnp.int32) // 16)[None, :], 0), axis=1
    )
    key_group = jnp.broadcast_to(
        block_group.astype(jnp.float32).reshape(4, 4, 1, 4, 1), (4, 4, 2, 4, 32)
    ).reshape(4, 1024)

    attended = call(
        attend_kernel,
        struct((512, 96)),
        [queries, keyed, valued, info, key_group, *prefix_pieces],
        scratch=[
            pltpu.VMEM((4, 256, 1024), jnp.float32),
            pltpu.VMEM((4, 1024, 96), jnp.bfloat16),
            pltpu.VMEM((4, 1024, 96), jnp.bfloat16),
        ],
    )
    attended = attended.reshape(2, 4, 64, 96)
    back = [attended[:, 0], to_pair(attended[:, 1], 1), to_pair(attended[:, 2], -1), to_pair(attended[:, 3], 2)]
    heads = []
    for h in range(4):
        at = jnp.where(zl == 0, h - zh, zh - h) % 4
        heads.append(
            jnp.where(at < 2, jnp.where(at == 0, back[0], back[1]), jnp.where(at == 2, back[3], back[2]))
        )
    home = jnp.concatenate(heads, axis=2)
    home_all = [home] + [mp_xor(home, k) for k in (1, 2, 3)]

    out_weight = call(order_kernel, struct((4, 4, 4, 48, 384)), [pos, *out_pieces], scalars=1)
    hidden = call(
        out_kernel, struct((64, 1536)), [pos, *home_all, out_weight, lengths[:, None]], scalars=1
    ).reshape(64, 2, 768)
    suffix_cache = call(unpack_kernel, struct((64, 1536)), [received]).reshape(64, 2, 2, 384)
    return hidden, suffix_cache


def solution(mesh):
    in_specs = (
        P("dp", None, None),
        P(),
        P("dp", "mp"),
        P("dp", "mp"),
        P("dp", "mp"),
        P("dp", "mp"),
        P("dp", None, None, "mp"),
        P("dp"),
        P("dp"),
        P("dp"),
        P(),
    )
    out_specs = (P("dp", None, "mp"), P("dp", None, None, "mp"))
    return jax.shard_map(on_device, mesh=mesh, in_specs=in_specs, out_specs=out_specs, check_vma=False)
```

```python
import math

import jax
import jax.numpy as jnp
import numpy as np
from jax import lax
from jax.experimental import pallas as pl
from jax.experimental.pallas import tpu as pltpu
from jax.sharding import PartitionSpec as P


HD = 96
PREFIX = 1024
NEG = -1e30


def place(dp, m):
    return dp // 16, (dp // 4) % 4, dp % 4, m // 2, m % 2


def index_of(y, zh, x, zl, core):
    return ((y % 4) * 16 + (zh % 4) * 4 + x % 4) * 4 + zl * 2 + core


def move(value, where):
    perm = []
    for dp in range(64):
        for m in range(4):
            perm.append((dp * 4 + m, index_of(*where(*place(dp, m)))))
    return lax.ppermute(value, ("dp", "mp"), perm)


def shift(value, axis, k):
    step = {"y": (k, 0, 0), "zh": (0, k, 0), "x": (0, 0, k)}[axis]
    return move(value, lambda y, zh, x, zl, core: (y + step[0], zh + step[1], x + step[2], zl, core))


def mp_xor(value, mask):
    return move(value, lambda y, zh, x, zl, core: (y, zh, x, zl ^ (mask // 2), core ^ (mask % 2)))


def swap_y_mp(value):
    return move(value, lambda y, zh, x, zl, core: (2 * zl + core, zh, x, y // 2, y % 2))


def next_chip(value):
    return move(value, lambda y, zh, x, zl, core: (y, zh + 1 if zl else zh - 1, x, 1 - zl, core))


def to_pair(value, side):
    return move(value, lambda y, zh, x, zl, core: (y, zh + side if zl else zh - side, x, zl, core))


def dot_nt(a, b):
    return lax.dot_general(a, b, (((1,), (1,)), ((), ())), preferred_element_type=jnp.float32)


def dot_tn(a, b):
    return lax.dot_general(a, b, (((0,), (0,)), ((), ())), preferred_element_type=jnp.float32)


def rope_tables():
    position = (PREFIX + np.arange(2)).astype(np.float32)
    frequency = np.float32(10000.0) ** (-np.arange(HD // 2).astype(np.float32) * np.float32(2.0) / np.float32(HD))
    angles = position[:, None] * frequency.astype(np.float32)[None, :]
    angles = np.concatenate([angles, angles], axis=-1).astype(np.float32)
    return np.cos(angles).astype(np.float32), np.sin(angles).astype(np.float32)


def qkv_kernel(
    pos_ref, own_ref, oth_ref, w0, w1, w2, w3, cos_ref, sin_ref,
    q_out, k_out, v_out, info_out, send_out, wsc,
):
    y, zh, x, c = pos_ref[0], pos_ref[1], pos_ref[2], pos_ref[3]
    for kx, piece in enumerate((w0, w1, w2, w3)):
        xa = (x - kx) & 3
        for kz in range(4):
            for ky in range(4):
                wsc[(y - ky) & 3, (zh - kz) & 3, xa] = piece[ky, :, 288 * kz : 288 * kz + 288]
    rhs = wsc[...].reshape(3072, 288)
    accs = [
        jnp.dot(ref[:, :, 0:3072].reshape(256, 3072), rhs, preferred_element_type=jnp.float32)
        for ref in (own_ref, oth_ref)
    ]
    first = c == 0
    slots = (jnp.where(first, accs[0], accs[1]), jnp.where(first, accs[1], accs[0]))

    def rotate(values, t):
        turned = jnp.concatenate([-values[:, 48:], values[:, :48]], axis=1)
        return (values * cos_ref[t : t + 1, :] + turned * sin_ref[t : t + 1, :]).astype(jnp.bfloat16)

    info = own_ref[:, :, 3072:3200].reshape(256, 128).astype(jnp.float32)
    info_out[...] = info
    live = info[:, 2:3] > 1.5
    parts = []
    for t in range(2):
        rows = pl.ds(256 * t, 256)
        q_out[rows, :] = rotate(slots[t][:, :96], t)
        keyed = rotate(slots[t][:, 96:192], t)
        valued = slots[t][:, 192:288].astype(jnp.bfloat16)
        k_out[rows, :] = keyed
        v_out[rows, :] = valued
        if t == 1:
            keyed = jnp.where(live, keyed.astype(jnp.float32), 0.0).astype(jnp.bfloat16)
            valued = jnp.where(live, valued.astype(jnp.float32), 0.0).astype(jnp.bfloat16)
        parts += [keyed, valued]
    packed = jnp.concatenate(parts, axis=1)
    dest_iota = lax.broadcasted_iota(jnp.int32, (64, 64), 1).astype(jnp.float32)
    lane_iota = lax.broadcasted_iota(jnp.int32, (64, 128), 1)
    extras = jnp.zeros((64, 128), jnp.float32)
    for ky in range(4):
        block = info[64 * ky : 64 * ky + 64]
        pick = jnp.where(block[:, 0:1] == dest_iota, 1.0, 0.0).astype(jnp.bfloat16)
        moved = dot_tn(pick, packed[64 * ky : 64 * ky + 64])
        send_out[:, ky // 2, 384 * (ky % 2) : 384 * (ky % 2) + 384] = moved.astype(jnp.bfloat16)
        slot = jnp.where(lane_iota == ky, block[:, 1:2], 0.0).astype(jnp.bfloat16)
        extras = extras + dot_tn(pick, slot)
    for half in range(2):
        send_out[:, half, 768:896] = extras.astype(jnp.bfloat16)


def attend_kernel(q_ref, k_ref, v_ref, info_ref, kg_ref, p0, p1, p2, p3, out_ref, s_ref, keys_ref, values_ref):
    factor = math.log2(math.e) / math.sqrt(HD)
    for kz in range(4):
        for ky, piece in enumerate((p0, p1, p2, p3)):
            for half in range(2):
                rows = pl.ds(256 * ky + 128 * half, 128)
                lane = 384 * kz + 192 * half
                keys_ref[kz, rows, :] = piece[:, :, lane : lane + 96].reshape(128, 96)
                values_ref[kz, rows, :] = piece[:, :, lane + 96 : lane + 192].reshape(128, 96)
    group = info_ref[:, 3:4]
    live = info_ref[:, 2:3] > 1.5

    def one_slot(t):
        rows = pl.ds(256 * t, 256)
        queries = q_ref[rows, :]
        wide = queries.astype(jnp.float32)
        first = jnp.sum(wide * k_ref[0:256, :].astype(jnp.float32), axis=1, keepdims=True)
        second = jnp.sum(wide * k_ref[256:512, :].astype(jnp.float32), axis=1, keepdims=True)
        second = jnp.where(live, second, NEG) if t == 1 else jnp.full_like(second, NEG)

        def score(ky, top):
            scores = dot_nt(queries, keys_ref[ky])
            scores = jnp.where(group == kg_ref[ky : ky + 1, :], scores, NEG)
            s_ref[ky] = scores
            return jnp.maximum(top, jnp.max(scores, axis=1, keepdims=True))

        top = jnp.maximum(first, second)
        for kz in range(4):
            top = score(kz, top)
        total = jnp.zeros((256, 1), jnp.float32)
        acc = jnp.zeros((256, 96), jnp.float32)
        for i, value in enumerate((first, second)):
            weight = jnp.exp2((value - top) * factor)
            total = total + weight
            values = v_ref[256 * i : 256 * i + 256, :].astype(jnp.float32)
            acc = acc + weight.astype(jnp.bfloat16).astype(jnp.float32) * values

        def gather(ky, state):
            total, acc = state
            weights = jnp.exp2((s_ref[ky] - top) * factor)
            total = total + jnp.sum(weights, axis=1, keepdims=True)
            acc = acc + jnp.dot(
                weights.astype(jnp.bfloat16), values_ref[ky], preferred_element_type=jnp.float32
            )
            return total, acc

        for kz in range(4):
            total, acc = gather(kz, (total, acc))
        out_ref[rows, :] = (acc / total).astype(jnp.bfloat16)

    for t in range(2):
        one_slot(t)


def order_kernel(pos_ref, w0, w1, w2, w3, out_ref):
    y, zh, x = pos_ref[0], pos_ref[1], pos_ref[2]
    for ky, piece in enumerate((w0, w1, w2, w3)):
        for kx in range(4):
            for kz in range(4):
                out_ref[(y - ky) & 3, (zh - kz) & 3, (x - kx) & 3] = piece[kx, :, 384 * kz : 384 * kz + 384]


def out_kernel(pos_ref, a0, a1, a2, a3, w_ref, len_ref, out_ref):
    m = pos_ref[4]
    acc = None
    for k, block in enumerate((a0, a1, a2, a3)):
        weight = w_ref[m ^ k].reshape(768, 384)
        part = dot_nt(block[...].reshape(128, 384), weight)
        acc = part if acc is None else acc + part
    out_ref[:, 0, :] = acc[0:64].astype(jnp.bfloat16)
    out_ref[:, 1, :] = jnp.where(len_ref[...] > 1, acc[64:128], 0.0).astype(jnp.bfloat16)


def unpack_kernel(recv_ref, out_ref):
    slot_iota = lax.broadcasted_iota(jnp.int32, (256, 64), 1).astype(jnp.float32)
    source_head = (lax.broadcasted_iota(jnp.int32, (256, 1), 0) // 4) % 4
    data = jnp.concatenate(
        [recv_ref[:, k // 2, 384 * (k % 2) : 384 * (k % 2) + 384] for k in range(4)], axis=0
    )
    tail = recv_ref[:, 0, 768:896].astype(jnp.float32)
    slots = jnp.concatenate([tail[:, k : k + 1] for k in range(4)], axis=0)
    moved = []
    for head in range(4):
        own = jnp.where(source_head == head, slots, -1.0)
        pick = jnp.where(own == slot_iota, 1.0, 0.0).astype(jnp.bfloat16)
        moved.append(dot_tn(pick, data).astype(jnp.bfloat16))
    for part in range(4):
        row = jnp.concatenate([one[:, 96 * part : 96 * part + 96] for one in moved], axis=1)
        out_ref[:, part // 2, part % 2, :] = row


def call(kernel, outs, inputs, scratch=(), scalars=0):
    vmem = pl.BlockSpec(memory_space=pltpu.VMEM)
    smem = pl.BlockSpec(memory_space=pltpu.SMEM)
    single = not isinstance(outs, (list, tuple))
    return pl.pallas_call(
        kernel,
        out_shape=outs,
        in_specs=[smem] * scalars + [vmem] * (len(inputs) - scalars),
        out_specs=vmem if single else [vmem] * len(outs),
        scratch_shapes=list(scratch),
    )(*inputs)


def struct(shape, dtype=jnp.bfloat16):
    return jax.ShapeDtypeStruct(shape, dtype)


def spread(value, axis):
    return [value] + [shift(value, axis, k) for k in (1, 2, 3)]


def on_device(
    tokens, norm_gain_vector, query_weight, key_weight, value_weight, output_weight,
    prefix_cache, lengths, groups, deal_slot, owners,
):
    dp = lax.axis_index("dp")
    m = lax.axis_index("mp")
    y, zh, x, c = dp // 16, (dp // 4) % 4, dp % 4, m % 2
    pos = jnp.stack([y, zh, x, c, m]).astype(jnp.int32)

    zl = m // 2
    block = prefix_cache[0]
    blank = jnp.zeros((48, 96), jnp.bfloat16)
    by_head = []
    for h in range(4):
        cols = slice(96 * h, 96 * h + 96)
        projections = [w[:, cols] for w in (query_weight, key_weight, value_weight)]
        pairs = [block[r : r + 32, kind, cols] for r in (0, 32) for kind in (0, 1)]
        by_head.append(
            jnp.concatenate(
                [jnp.concatenate([*projections, blank], axis=1), jnp.concatenate(pairs, axis=1)], axis=0
            )
        )
    by_head = jnp.stack(by_head)
    got = []
    for k in range(4):
        piece = lax.dynamic_index_in_dim(by_head, (zh + k) % 4, 0, keepdims=False)
        piece = jnp.concatenate([piece, output_weight], axis=0)
        got.append(piece if k == 0 else shift(piece, "zh", k))
    weight_rows = jnp.concatenate([g[0:48, 0:288] for g in got], axis=1)
    prefix_rows = jnp.concatenate([g[48:80] for g in got], axis=1)
    out_rows = jnp.concatenate([g[80:128] for g in got], axis=1)

    own = lax.dynamic_index_in_dim(tokens, c, 1, keepdims=False).astype(jnp.float32)
    scale = lax.rsqrt(jnp.mean(own * own, axis=-1, keepdims=True) + 1e-05)
    normed = (own * scale * norm_gain_vector).astype(jnp.bfloat16)
    extras = jnp.stack([deal_slot // 64, deal_slot % 64, lengths, groups], axis=1).astype(jnp.bfloat16)
    extras = jnp.pad(extras, ((0, 0), (0, 124)))
    sent = jnp.concatenate([normed, extras], axis=1)
    outer = next_chip(sent)
    inner = mp_xor(outer, 2)
    far = next_chip(inner)
    own_rows = jnp.stack([sent, outer, inner, far])
    other_rows = mp_xor(own_rows, 1)

    weight_pieces = spread(jnp.stack(spread(weight_rows, "y")), "x")
    prefix_pieces = spread(jnp.stack(spread(prefix_rows, "x")), "y")
    out_pieces = spread(jnp.stack(spread(swap_y_mp(out_rows), "x")), "y")

    cosine, sine = rope_tables()
    queries, keyed, valued, info, send = call(
        qkv_kernel,
        [struct((512, 96)), struct((512, 96)), struct((512, 96)), struct((256, 128), jnp.float32), struct((64, 2, 896))],
        [pos, own_rows, other_rows, *weight_pieces, jnp.asarray(cosine), jnp.asarray(sine)],
        scratch=[pltpu.VMEM((4, 4, 4, 48, 288), jnp.bfloat16)],
        scalars=1,
    )
    received = lax.all_to_all(send, "dp", split_axis=0, concat_axis=0, tiled=True)

    r4 = jnp.arange(4, dtype=jnp.int32)
    source = (
        ((zh - r4) % 4)[:, None, None] * 4 + ((y - r4) % 4)[None, :, None] * 16 + ((x - r4) % 4)[None, None, :]
    ).reshape(64)
    block_group = jnp.sum(
        jnp.where(owners[None, :] == source[:, None], (jnp.arange(64, dtype=jnp.int32) // 16)[None, :], 0), axis=1
    )
    key_group = jnp.broadcast_to(
        block_group.astype(jnp.float32).reshape(4, 4, 1, 4, 1), (4, 4, 2, 4, 32)
    ).reshape(4, 1024)

    attended = call(
        attend_kernel,
        struct((512, 96)),
        [queries, keyed, valued, info, key_group, *prefix_pieces],
        scratch=[
            pltpu.VMEM((4, 256, 1024), jnp.float32),
            pltpu.VMEM((4, 1024, 96), jnp.bfloat16),
            pltpu.VMEM((4, 1024, 96), jnp.bfloat16),
        ],
    )
    attended = attended.reshape(2, 4, 64, 96)
    back = [attended[:, 0], to_pair(attended[:, 1], 1), to_pair(attended[:, 2], -1), to_pair(attended[:, 3], 2)]
    heads = []
    for h in range(4):
        at = jnp.where(zl == 0, h - zh, zh - h) % 4
        heads.append(
            jnp.where(at < 2, jnp.where(at == 0, back[0], back[1]), jnp.where(at == 2, back[3], back[2]))
        )
    home = jnp.concatenate(heads, axis=2)
    home_all = [home] + [mp_xor(home, k) for k in (1, 2, 3)]

    out_weight = call(order_kernel, struct((4, 4, 4, 48, 384)), [pos, *out_pieces], scalars=1)
    hidden = call(out_kernel, struct((64, 2, 768)), [pos, *home_all, out_weight, lengths[:, None]], scalars=1)
    suffix_cache = call(unpack_kernel, struct((64, 2, 2, 384)), [received])
    return hidden, suffix_cache


def solution(mesh):
    in_specs = (
        P("dp", None, None),
        P(),
        P("dp", "mp"),
        P("dp", "mp"),
        P("dp", "mp"),
        P("dp", "mp"),
        P("dp", None, None, "mp"),
        P("dp"),
        P("dp"),
        P("dp"),
        P(),
    )
    out_specs = (P("dp", None, "mp"), P("dp", None, None, "mp"))
    return jax.shard_map(on_device, mesh=mesh, in_specs=in_specs, out_specs=out_specs, check_vma=False)
```

```python
import math

import jax
import jax.numpy as jnp
import numpy as np
from jax import lax
from jax.experimental import pallas as pl
from jax.experimental.pallas import tpu as pltpu
from jax.sharding import PartitionSpec as P


HD = 96
PREFIX = 1024
NEG = -1e30


def place(dp, m):
    return dp // 16, (dp // 4) % 4, dp % 4, m // 2, m % 2


def index_of(y, zh, x, zl, core):
    return ((y % 4) * 16 + (zh % 4) * 4 + x % 4) * 4 + zl * 2 + core


def move(value, where):
    perm = []
    for dp in range(64):
        for m in range(4):
            perm.append((dp * 4 + m, index_of(*where(*place(dp, m)))))
    return lax.ppermute(value, ("dp", "mp"), perm)


def shift(value, axis, k):
    step = {"y": (k, 0, 0), "zh": (0, k, 0), "x": (0, 0, k)}[axis]
    return move(value, lambda y, zh, x, zl, core: (y + step[0], zh + step[1], x + step[2], zl, core))


def mp_xor(value, mask):
    return move(value, lambda y, zh, x, zl, core: (y, zh, x, zl ^ (mask // 2), core ^ (mask % 2)))


def swap_y_mp(value):
    return move(value, lambda y, zh, x, zl, core: (2 * zl + core, zh, x, y // 2, y % 2))


def next_chip(value):
    return move(value, lambda y, zh, x, zl, core: (y, zh + 1 if zl else zh - 1, x, 1 - zl, core))


def to_pair(value, side):
    return move(value, lambda y, zh, x, zl, core: (y, zh + side if zl else zh - side, x, zl, core))


def dot_nt(a, b):
    return lax.dot_general(a, b, (((1,), (1,)), ((), ())), preferred_element_type=jnp.float32)


def dot_tn(a, b):
    return lax.dot_general(a, b, (((0,), (0,)), ((), ())), preferred_element_type=jnp.float32)


def rope_tables():
    position = (PREFIX + np.arange(2)).astype(np.float32)
    frequency = np.float32(10000.0) ** (-np.arange(HD // 2).astype(np.float32) * np.float32(2.0) / np.float32(HD))
    angles = position[:, None] * frequency.astype(np.float32)[None, :]
    angles = np.concatenate([angles, angles], axis=-1).astype(np.float32)
    return np.cos(angles).astype(np.float32), np.sin(angles).astype(np.float32)


def qkv_kernel(
    pos_ref, own_ref, oth_ref, w0, w1, w2, w3, cos_ref, sin_ref,
    q_out, k_out, v_out, info_out, send_out, wsc,
):
    y, zh, x, c = pos_ref[0], pos_ref[1], pos_ref[2], pos_ref[3]
    for kx, piece in enumerate((w0, w1, w2, w3)):
        xa = (x - kx) & 3
        for kz in range(4):
            for ky in range(4):
                wsc[(y - ky) & 3, (zh - kz) & 3, xa] = piece[ky, :, 288 * kz : 288 * kz + 288]
    rhs = wsc[...].reshape(3072, 288)
    accs = [
        jnp.dot(ref[:, :, 0:3072].reshape(256, 3072), rhs, preferred_element_type=jnp.float32)
        for ref in (own_ref, oth_ref)
    ]
    first = c == 0
    slots = (jnp.where(first, accs[0], accs[1]), jnp.where(first, accs[1], accs[0]))

    def rotate(values, t):
        turned = jnp.concatenate([-values[:, 48:], values[:, :48]], axis=1)
        return (values * cos_ref[t : t + 1, :] + turned * sin_ref[t : t + 1, :]).astype(jnp.bfloat16)

    info = own_ref[:, :, 3072:3200].reshape(256, 128).astype(jnp.float32)
    info_out[...] = info
    live = info[:, 2:3] > 1.5
    parts = []
    for t in range(2):
        rows = pl.ds(256 * t, 256)
        q_out[rows, :] = rotate(slots[t][:, :96], t)
        keyed = rotate(slots[t][:, 96:192], t)
        valued = slots[t][:, 192:288].astype(jnp.bfloat16)
        k_out[rows, :] = keyed
        v_out[rows, :] = valued
        if t == 1:
            keyed = jnp.where(live, keyed.astype(jnp.float32), 0.0).astype(jnp.bfloat16)
            valued = jnp.where(live, valued.astype(jnp.float32), 0.0).astype(jnp.bfloat16)
        parts += [keyed, valued]
    packed = jnp.concatenate(parts, axis=1)
    dest_iota = lax.broadcasted_iota(jnp.int32, (64, 64), 1).astype(jnp.float32)
    lane_iota = lax.broadcasted_iota(jnp.int32, (64, 128), 1)
    extras = jnp.zeros((64, 128), jnp.float32)
    for ky in range(4):
        block = info[64 * ky : 64 * ky + 64]
        pick = jnp.where(block[:, 0:1] == dest_iota, 1.0, 0.0).astype(jnp.bfloat16)
        moved = dot_tn(pick, packed[64 * ky : 64 * ky + 64])
        send_out[:, ky // 2, 384 * (ky % 2) : 384 * (ky % 2) + 384] = moved.astype(jnp.bfloat16)
        slot = jnp.where(lane_iota == ky, block[:, 1:2], 0.0).astype(jnp.bfloat16)
        extras = extras + dot_tn(pick, slot)
    for half in range(2):
        send_out[:, half, 768:896] = extras.astype(jnp.bfloat16)


def attend_kernel(q_ref, k_ref, v_ref, info_ref, kg_ref, p0, p1, p2, p3, out_ref, s_ref, keys_ref, values_ref):
    factor = math.log2(math.e) / math.sqrt(HD)
    for kz in range(4):
        for ky, piece in enumerate((p0, p1, p2, p3)):
            for half in range(2):
                rows = pl.ds(256 * ky + 128 * half, 128)
                lane = 384 * kz + 192 * half
                keys_ref[kz, rows, :] = piece[:, :, lane : lane + 96].reshape(128, 96)
                values_ref[kz, rows, :] = piece[:, :, lane + 96 : lane + 192].reshape(128, 96)
    group = info_ref[:, 3:4]
    live = info_ref[:, 2:3] > 1.5

    def one_slot(t):
        rows = pl.ds(256 * t, 256)
        queries = q_ref[rows, :]
        wide = queries.astype(jnp.float32)
        first = jnp.sum(wide * k_ref[0:256, :].astype(jnp.float32), axis=1, keepdims=True)
        second = jnp.sum(wide * k_ref[256:512, :].astype(jnp.float32), axis=1, keepdims=True)
        second = jnp.where(live, second, NEG) if t == 1 else jnp.full_like(second, NEG)

        def score(ky, top):
            scores = dot_nt(queries, keys_ref[ky])
            scores = jnp.where(group == kg_ref[ky : ky + 1, :], scores, NEG)
            s_ref[ky] = scores
            return jnp.maximum(top, jnp.max(scores, axis=1, keepdims=True))

        top = jnp.maximum(first, second)
        for kz in range(4):
            top = score(kz, top)
        total = jnp.zeros((256, 1), jnp.float32)
        acc = jnp.zeros((256, 96), jnp.float32)
        for i, value in enumerate((first, second)):
            weight = jnp.exp2((value - top) * factor)
            total = total + weight
            values = v_ref[256 * i : 256 * i + 256, :].astype(jnp.float32)
            acc = acc + weight.astype(jnp.bfloat16).astype(jnp.float32) * values

        def gather(ky, state):
            total, acc = state
            weights = jnp.exp2((s_ref[ky] - top) * factor)
            total = total + jnp.sum(weights, axis=1, keepdims=True)
            acc = acc + jnp.dot(
                weights.astype(jnp.bfloat16), values_ref[ky], preferred_element_type=jnp.float32
            )
            return total, acc

        for kz in range(4):
            total, acc = gather(kz, (total, acc))
        out_ref[rows, :] = (acc / total).astype(jnp.bfloat16)

    for t in range(2):
        one_slot(t)


def out_kernel(pos_ref, a0, a1, a2, a3, w0, w1, w2, w3, dest_ref, len_ref, out_ref, att_ref):
    y, m = pos_ref[0], pos_ref[4]
    for k, block in enumerate((a0, a1, a2, a3)):
        att_ref[m ^ k] = block[...].reshape(128, 384)
    parts = [None] * 4
    for ky, piece in enumerate((w0, w1, w2, w3)):
        rows = att_ref[(y - ky) & 3]
        for kz in range(4):
            weight = piece[:, :, 384 * kz : 384 * kz + 384].reshape(192, 384)
            part = dot_nt(rows, weight)
            parts[kz] = part if parts[kz] is None else parts[kz] + part
    column = lax.broadcasted_iota(jnp.int32, (192, 768), 1).astype(jnp.float32)
    acc = None
    for kz in range(4):
        pick = jnp.where(dest_ref[192 * kz : 192 * kz + 192, :] == column, 1.0, 0.0).astype(jnp.bfloat16)
        part = jnp.dot(parts[kz].astype(jnp.bfloat16), pick, preferred_element_type=jnp.float32)
        acc = part if acc is None else acc + part
    out_ref[:, 0, :] = acc[0:64].astype(jnp.bfloat16)
    out_ref[:, 1, :] = jnp.where(len_ref[...] > 1, acc[64:128], 0.0).astype(jnp.bfloat16)


def unpack_kernel(recv_ref, out_ref):
    slot_iota = lax.broadcasted_iota(jnp.int32, (256, 64), 1).astype(jnp.float32)
    source_head = (lax.broadcasted_iota(jnp.int32, (256, 1), 0) // 4) % 4
    data = jnp.concatenate(
        [recv_ref[:, k // 2, 384 * (k % 2) : 384 * (k % 2) + 384] for k in range(4)], axis=0
    )
    tail = recv_ref[:, 0, 768:896].astype(jnp.float32)
    slots = jnp.concatenate([tail[:, k : k + 1] for k in range(4)], axis=0)
    moved = []
    for head in range(4):
        own = jnp.where(source_head == head, slots, -1.0)
        pick = jnp.where(own == slot_iota, 1.0, 0.0).astype(jnp.bfloat16)
        moved.append(dot_tn(pick, data).astype(jnp.bfloat16))
    for part in range(4):
        row = jnp.concatenate([one[:, 96 * part : 96 * part + 96] for one in moved], axis=1)
        out_ref[:, part // 2, part % 2, :] = row


def call(kernel, outs, inputs, scratch=(), scalars=0):
    vmem = pl.BlockSpec(memory_space=pltpu.VMEM)
    smem = pl.BlockSpec(memory_space=pltpu.SMEM)
    single = not isinstance(outs, (list, tuple))
    return pl.pallas_call(
        kernel,
        out_shape=outs,
        in_specs=[smem] * scalars + [vmem] * (len(inputs) - scalars),
        out_specs=vmem if single else [vmem] * len(outs),
        scratch_shapes=list(scratch),
    )(*inputs)


def struct(shape, dtype=jnp.bfloat16):
    return jax.ShapeDtypeStruct(shape, dtype)


def spread(value, axis):
    return [value] + [shift(value, axis, k) for k in (1, 2, 3)]


def on_device(
    tokens, norm_gain_vector, query_weight, key_weight, value_weight, output_weight,
    prefix_cache, lengths, groups, deal_slot, owners,
):
    dp = lax.axis_index("dp")
    m = lax.axis_index("mp")
    y, zh, x, c = dp // 16, (dp // 4) % 4, dp % 4, m % 2
    pos = jnp.stack([y, zh, x, c, m]).astype(jnp.int32)

    zl = m // 2
    block = prefix_cache[0]
    blank = jnp.zeros((48, 96), jnp.bfloat16)
    by_head = []
    for h in range(4):
        cols = slice(96 * h, 96 * h + 96)
        projections = [w[:, cols] for w in (query_weight, key_weight, value_weight)]
        pairs = [block[r : r + 32, kind, cols] for r in (0, 32) for kind in (0, 1)]
        by_head.append(
            jnp.concatenate(
                [jnp.concatenate([*projections, blank], axis=1), jnp.concatenate(pairs, axis=1)], axis=0
            )
        )
    by_head = jnp.stack(by_head)
    got = []
    for k in range(4):
        piece = lax.dynamic_index_in_dim(by_head, (zh + k) % 4, 0, keepdims=False)
        piece = jnp.concatenate([piece, output_weight], axis=0)
        got.append(piece if k == 0 else shift(piece, "zh", k))
    weight_rows = jnp.concatenate([g[0:48, 0:288] for g in got], axis=1)
    prefix_rows = jnp.concatenate([g[48:80] for g in got], axis=1)
    out_rows = jnp.concatenate([g[80:128] for g in got], axis=1)

    own = lax.dynamic_index_in_dim(tokens, c, 1, keepdims=False).astype(jnp.float32)
    scale = lax.rsqrt(jnp.mean(own * own, axis=-1, keepdims=True) + 1e-05)
    normed = (own * scale * norm_gain_vector).astype(jnp.bfloat16)
    extras = jnp.stack([deal_slot // 64, deal_slot % 64, lengths, groups], axis=1).astype(jnp.bfloat16)
    extras = jnp.pad(extras, ((0, 0), (0, 124)))
    sent = jnp.concatenate([normed, extras], axis=1)
    outer = next_chip(sent)
    inner = mp_xor(outer, 2)
    far = next_chip(inner)
    own_rows = jnp.stack([sent, outer, inner, far])
    other_rows = mp_xor(own_rows, 1)

    weight_pieces = spread(jnp.stack(spread(weight_rows, "y")), "x")
    prefix_pieces = spread(jnp.stack(spread(prefix_rows, "x")), "y")
    out_pieces = spread(jnp.stack(spread(swap_y_mp(out_rows), "x")), "y")

    cosine, sine = rope_tables()
    queries, keyed, valued, info, send = call(
        qkv_kernel,
        [struct((512, 96)), struct((512, 96)), struct((512, 96)), struct((256, 128), jnp.float32), struct((64, 2, 896))],
        [pos, own_rows, other_rows, *weight_pieces, jnp.asarray(cosine), jnp.asarray(sine)],
        scratch=[pltpu.VMEM((4, 4, 4, 48, 288), jnp.bfloat16)],
        scalars=1,
    )
    received = lax.all_to_all(send, "dp", split_axis=0, concat_axis=0, tiled=True)

    r4 = jnp.arange(4, dtype=jnp.int32)
    source = (
        ((zh - r4) % 4)[:, None, None] * 4 + ((y - r4) % 4)[None, :, None] * 16 + ((x - r4) % 4)[None, None, :]
    ).reshape(64)
    block_group = jnp.sum(
        jnp.where(owners[None, :] == source[:, None], (jnp.arange(64, dtype=jnp.int32) // 16)[None, :], 0), axis=1
    )
    key_group = jnp.broadcast_to(
        block_group.astype(jnp.float32).reshape(4, 4, 1, 4, 1), (4, 4, 2, 4, 32)
    ).reshape(4, 1024)

    attended = call(
        attend_kernel,
        struct((512, 96)),
        [queries, keyed, valued, info, key_group, *prefix_pieces],
        scratch=[
            pltpu.VMEM((4, 256, 1024), jnp.float32),
            pltpu.VMEM((4, 1024, 96), jnp.bfloat16),
            pltpu.VMEM((4, 1024, 96), jnp.bfloat16),
        ],
    )
    attended = attended.reshape(2, 4, 64, 96)
    back = [attended[:, 0], to_pair(attended[:, 1], 1), to_pair(attended[:, 2], -1), to_pair(attended[:, 3], 2)]
    heads = []
    for h in range(4):
        at = jnp.where(zl == 0, h - zh, zh - h) % 4
        heads.append(
            jnp.where(at < 2, jnp.where(at == 0, back[0], back[1]), jnp.where(at == 2, back[3], back[2]))
        )
    home = jnp.concatenate(heads, axis=2)
    home_all = [home] + [mp_xor(home, k) for k in (1, 2, 3)]

    row = np.arange(768, dtype=np.int32)
    place_of = (
        ((zh - row // 192) % 4) * 192 + ((x - (row // 48) % 4) % 4) * 48 + row % 48
    ).astype(jnp.float32)[:, None]
    hidden = call(
        out_kernel,
        struct((64, 2, 768)),
        [pos, *home_all, *out_pieces, place_of, lengths[:, None]],
        scratch=[pltpu.VMEM((4, 128, 384), jnp.bfloat16)],
        scalars=1,
    )
    suffix_cache = call(unpack_kernel, struct((64, 2, 2, 384)), [received])
    return hidden, suffix_cache


def solution(mesh):
    in_specs = (
        P("dp", None, None),
        P(),
        P("dp", "mp"),
        P("dp", "mp"),
        P("dp", "mp"),
        P("dp", "mp"),
        P("dp", None, None, "mp"),
        P("dp"),
        P("dp"),
        P("dp"),
        P(),
    )
    out_specs = (P("dp", None, "mp"), P("dp", None, None, "mp"))
    return jax.shard_map(on_device, mesh=mesh, in_specs=in_specs, out_specs=out_specs, check_vma=False)
```
